512 devices in a mesh: row: 32 (over x_hi, y, core), frame: 16 (over z, x_lo).
Axes of the slice: x: 4 (x_hi: 2, x_lo: 2; x = x_hi * 2 + x_lo), y: 8, z: 8, core: 2. Of those that a mesh axis runs over, the one named last changes fastest.
Arguments:
- frames: bfloat16 [64, 64, 256, 128], P('frame', None, 'row'), may hold values from -6 to 6
- w_pair: bfloat16 [3, 3, 64, 128], replicated, may hold values from -0.1875 to 0.1875
- w_mixed: bfloat16 [3, 3, 64, 64], replicated, may hold values from -0.25 to 0.25
- slope_pair: float32 [64], replicated, may hold values from 0.05 to 0.5
- slope_mixed: float32 [64], replicated, may hold values from 0.05 to 0.5
Outputs:
- merged: bfloat16 [16, 64, 256, 128], P('frame', None, 'row')
The draws below stay inside these ranges and needn't reach their ends.
All inputs are finite; a program needn't handle non-finite values.
Results may differ from the reference program's by a relative error of at most 0.0051.
Values may be sent and summed in bfloat16 or wider, within the bound.
No kernel may reach another device: no remote copies, remote signals or barrier semaphores. Data moves between devices by JAX's collectives and lax.ppermute only.
A program may use at most 64 MiB of HBM per device.

```python
import jax
import jax.numpy as jnp
from jax import lax

C = 64
W = 128
FRAMES = 64
H = 256


def shard_levels(stream_key, shape, cuts, smallest, top_value):
    loudness, own = 1.0, jax.random.fold_in(stream_key, 6)
    for axis_at, parts in cuts:
        steps = jnp.exp(jax.random.uniform(jax.random.fold_in(own, axis_at), (parts,), jnp.float32, smallest / len(cuts), top_value / len(cuts)))
        loudness = loudness * jnp.repeat(steps, shape[axis_at] // parts).reshape([-1 if axis == axis_at else 1 for axis in range(len(shape))])
    return loudness


def bell_draw(stream_key, extent, deviation, reach, shards=(), dtype=jnp.bfloat16):
    values = deviation * jax.random.normal(stream_key, extent, jnp.float32)
    if shards:
        values = values * shard_levels(stream_key, extent, shards, -0.22, 0.18)
    return jnp.clip(values, -reach, reach).astype(dtype)


def setup_inputs(seed: int = 0) -> dict:
    streams_of = jax.random.split(jax.random.key(seed), 6)
    frames = bell_draw(streams_of[0], (FRAMES, C, H, W), 1.0, 6.0, ((0, 16), (2, 32)))
    w_pair = bell_draw(streams_of[1], (3, 3, C, 2 * C), (18 * C) ** -0.5, 0.1875)
    w_mixed = bell_draw(streams_of[2], (3, 3, C, C), (9 * C) ** -0.5, 0.25)
    slope_pair = jnp.clip(jax.random.uniform(streams_of[3], (C,), jnp.float32, 0.05, 0.5), 0.05, 0.5)
    slope_mixed = jnp.clip(jax.random.uniform(streams_of[4], (C,), jnp.float32, 0.05, 0.5), 0.05, 0.5)
    return {"frames": frames, "w_pair": w_pair, "w_mixed": w_mixed, "slope_pair": slope_pair, "slope_mixed": slope_mixed}


def prelu(values, slope):
    return jnp.where(values >= 0, values, slope[:, None, None] * values)


def convolve(image, weight):
    rows = image.shape[1]
    cols = image.shape[2]
    padded = jnp.pad(image.astype(jnp.float32), ((0, 0), (1, 1), (1, 1)))
    wide = weight.astype(jnp.float32)
    total = jnp.zeros((weight.shape[2], rows, cols), jnp.float32)
    for tap_y in range(3):
        for tap_x in range(3):
            total = total + jnp.einsum("oc,chw->ohw", wide[tap_y, tap_x], padded[:, tap_y:tap_y + rows, tap_x:tap_x + cols], precision=lax.Precision.HIGHEST)
    return total


def merge_pair(first, second, w_pair, w_mixed, slope_pair, slope_mixed):
    joined = jnp.concatenate([first, second], axis=0)
    hidden = prelu(convolve(joined, w_pair), slope_pair).astype(jnp.bfloat16)
    branch = prelu(convolve(hidden, w_mixed), slope_mixed)
    return (first.astype(jnp.float32) + branch).astype(jnp.bfloat16)


def reference(frames, w_pair, w_mixed, slope_pair, slope_mixed):
    def apply(pair):
        return merge_pair(pair[0], pair[1], w_pair, w_mixed, slope_pair, slope_mixed)

    half = FRAMES // 2
    quarter = FRAMES // 4
    level_one = lax.map(apply, (frames[:half], frames[half:]))
    level_two = lax.map(apply, (level_one[:quarter], level_one[quarter:]))
    grouped = level_two.reshape(FRAMES // 16, 4, C, H, W)
    return jnp.transpose(grouped, (1, 0, 2, 3, 4)).reshape(quarter, C, H, W)
```

```python
import jax
import jax.numpy as jnp
from jax import lax
from jax.experimental import pallas as pl
from jax.experimental.pallas import tpu as pltpu
from jax.sharding import PartitionSpec as P

ROWS = 8
HALO = 4
CH = 64
LANES = 128


def rows_first(stack):
    def body(src, top, bottom, wide):
        for slot, frame in enumerate((0, 2, 1, 3)):
            wide[...] = src[frame].astype(jnp.float32).reshape(CH * ROWS, LANES)
            for row in range(ROWS):
                value = wide[pl.ds(row, CH, stride=ROWS), :].astype(jnp.bfloat16)
                half = top if row < HALO else bottom
                half[row % HALO, slot * CH : (slot + 1) * CH, :] = value

    half = jax.ShapeDtypeStruct((HALO, 4 * CH, LANES), jnp.bfloat16)
    return pl.pallas_call(
        body,
        out_shape=(half, half),
        scratch_shapes=[pltpu.VMEM((CH * ROWS, LANES), jnp.float32)],
        name="rows_first",
    )(stack)


def merges(above, top, bottom, below, w_pair, w_mixed, slope_pair, slope_mixed):
    def body(above_r, top_r, bottom_r, below_r, wp_r, wm_r, sp_r, sm_r, out_r, hid, one, wide):
        place = lax.axis_index("row")
        last = lax.axis_size("row") - 1
        lane = lax.broadcasted_iota(jnp.int32, (CH, LANES), 1)
        not_first = lane > 0
        not_last = lane < LANES - 1
        square = lax.broadcasted_iota(jnp.int32, (CH, CH), 0) == lax.broadcasted_iota(jnp.int32, (CH, CH), 1)

        def column(slope):
            return jnp.sum(jnp.where(square, slope[...], 0.0), axis=1, keepdims=True)

        s_pair = column(sp_r)
        s_mixed = column(sm_r)
        lhs_pair = jnp.concatenate([wp_r[0], wp_r[1], wp_r[2]], axis=1)
        lhs_mixed = jnp.concatenate([wm_r[0], wm_r[1], wm_r[2]], axis=1)
        halves = (above_r, top_r, bottom_r, below_r)

        def frame_row(row, pair):
            return halves[row // HALO][row % HALO, pair * 2 * CH : (pair + 1) * 2 * CH, :]

        def inside(row, value):
            if row < HALO:
                return jnp.where(place > 0, value, 0.0)
            if row >= HALO + ROWS:
                return jnp.where(place < last, value, 0.0)
            return value

        def fold(part, slope):
            left = jnp.where(not_first, pltpu.roll(part[:CH], 1, 1), 0.0)
            right = jnp.where(not_last, pltpu.roll(part[2 * CH :], LANES - 1, 1), 0.0)
            total = part[CH : 2 * CH] + left + right
            return jnp.where(total >= 0, total, slope * total)

        def level(load, base, low, high, emit):
            for row in range(low - 1, high + 1, 2):
                rows = [load(r) for r in range(row - 1, row + 3)]
                rhs = jnp.concatenate(
                    [jnp.concatenate(rows[0:3], axis=0), jnp.concatenate(rows[1:4], axis=0)], axis=1
                )
                both = jnp.dot(lhs_pair, rhs, preferred_element_type=jnp.float32)
                for k in range(2):
                    value = fold(both[:, k * LANES : (k + 1) * LANES], s_pair)
                    hid[base + row + k] = inside(row + k, value).astype(jnp.bfloat16)
            for row in range(low, high, 2):
                rows = [hid[base + r] for r in range(row - 1, row + 3)]
                rhs = jnp.concatenate(
                    [jnp.concatenate(rows[0:3], axis=0), jnp.concatenate(rows[1:4], axis=0)], axis=1
                )
                both = jnp.dot(lhs_mixed, rhs, preferred_element_type=jnp.float32)
                for k in range(2):
                    emit(row + k, fold(both[:, k * LANES : (k + 1) * LANES], s_mixed))

        for pair in range(2):

            def emit_one(row, branch, pair=pair):
                first = frame_row(row, pair)[:CH].astype(jnp.float32)
                one[row, pair * CH : (pair + 1) * CH, :] = inside(row, first + branch).astype(jnp.bfloat16)

            level(lambda row, pair=pair: frame_row(row, pair), 16 * pair, 2, 14, emit_one)

        def emit_two(row, branch):
            first = one[row, :CH, :].astype(jnp.float32)
            wide[pl.ds(row - HALO, CH, stride=ROWS), :] = first + branch

        level(lambda row: one[row], 32, HALO, HALO + ROWS, emit_two)
        out_r[...] = wide[...].reshape(CH, ROWS, LANES).astype(jnp.bfloat16)

    return pl.pallas_call(
        body,
        out_shape=jax.ShapeDtypeStruct((CH, ROWS, LANES), jnp.bfloat16),
        scratch_shapes=[
            pltpu.VMEM((48, CH, LANES), jnp.bfloat16),
            pltpu.VMEM((16, 2 * CH, LANES), jnp.bfloat16),
            pltpu.VMEM((CH * ROWS, LANES), jnp.float32),
        ],
        name="merges",
    )(above, top, bottom, below, w_pair, w_mixed, slope_pair, slope_mixed)


def on_device(frames, w_pair, w_mixed, slope_pair, slope_mixed):
    count = lax.axis_size("frame")
    quarter = count // 4
    groups = [[a + quarter * b for b in range(4)] for a in range(quarter)]
    stack = lax.all_to_all(frames, "frame", 0, 0, axis_index_groups=groups, tiled=True)
    top, bottom = rows_first(stack)
    ends = lax.axis_size("row") - 1
    above = lax.ppermute(bottom, "row", [(i, i + 1) for i in range(ends)])
    below = lax.ppermute(top, "row", [(i + 1, i) for i in range(ends)])
    merged = merges(
        above,
        top,
        bottom,
        below,
        w_pair.reshape(3, 3 * CH, 2 * CH),
        w_mixed.reshape(3, 3 * CH, CH),
        slope_pair.reshape(1, CH),
        slope_mixed.reshape(1, CH),
    )
    return merged[None]


def solution(mesh):
    placed = (P("frame", None, "row", None), P(), P(), P(), P())
    return jax.shard_map(
        on_device,
        mesh=mesh,
        in_specs=placed,
        out_specs=P("frame", None, "row", None),
        check_vma=False,
    )
```

```python
import jax
import jax.numpy as jnp
from jax import lax
from jax.experimental import pallas as pl
from jax.experimental.pallas import tpu as pltpu
from jax.sharding import PartitionSpec as P

ROWS = 8
HALO = 4
CH = 64
LANES = 128


def rows_first(stack):
    def body(src, top, bottom, wide):
        for slot, frame in enumerate((0, 2, 1, 3)):
            wide[...] = src[frame].astype(jnp.float32).reshape(CH * ROWS, LANES)
            for row in range(ROWS):
                value = wide[pl.ds(row, CH, stride=ROWS), :].astype(jnp.bfloat16)
                half = top if row < HALO else bottom
                half[row % HALO, slot * CH : (slot + 1) * CH, :] = value

    half = jax.ShapeDtypeStruct((HALO, 4 * CH, LANES), jnp.bfloat16)
    return pl.pallas_call(
        body,
        out_shape=(half, half),
        in_specs=[pl.BlockSpec(memory_space=pltpu.VMEM)],
        out_specs=(pl.BlockSpec(memory_space=pltpu.VMEM),) * 2,
        scratch_shapes=[pltpu.VMEM((CH * ROWS, LANES), jnp.float32)],
        compiler_params=pltpu.CompilerParams(vmem_limit_bytes=8 << 20),
        name="rows_first",
    )(stack)


def merges(above, top, bottom, below, w_pair, w_mixed, slope_pair, slope_mixed):
    def body(above_r, top_r, bottom_r, below_r, wp_r, wm_r, sp_r, sm_r, out_r, hid, one, wide):
        place = lax.axis_index("row")
        last = lax.axis_size("row") - 1
        lane = lax.broadcasted_iota(jnp.int32, (CH, LANES), 1)
        not_first = lane > 0
        not_last = lane < LANES - 1
        square = lax.broadcasted_iota(jnp.int32, (CH, CH), 0) == lax.broadcasted_iota(jnp.int32, (CH, CH), 1)

        def column(slope):
            return jnp.sum(jnp.where(square, slope[...], 0.0), axis=1, keepdims=True)

        s_pair = column(sp_r)
        s_mixed = column(sm_r)
        lhs_pair = jnp.concatenate([wp_r[0], wp_r[1], wp_r[2]], axis=1)
        lhs_mixed = jnp.concatenate([wm_r[0], wm_r[1], wm_r[2]], axis=1)
        halves = (above_r, top_r, bottom_r, below_r)

        def frame_row(row, pair):
            return halves[row // HALO][row % HALO, pair * 2 * CH : (pair + 1) * 2 * CH, :]

        def inside(row, value):
            if row < HALO:
                return jnp.where(place > 0, value, 0.0)
            if row >= HALO + ROWS:
                return jnp.where(place < last, value, 0.0)
            return value

        def fold(part, slope):
            left = jnp.where(not_first, pltpu.roll(part[:CH], 1, 1), 0.0)
            right = jnp.where(not_last, pltpu.roll(part[2 * CH :], LANES - 1, 1), 0.0)
            total = part[CH : 2 * CH] + left + right
            return jnp.where(total >= 0, total, slope * total)

        def level(load, base, low, high, emit):
            for row in range(low - 1, high + 1, 2):
                rows = [load(r) for r in range(row - 1, row + 3)]
                rhs = jnp.concatenate(
                    [jnp.concatenate(rows[0:3], axis=0), jnp.concatenate(rows[1:4], axis=0)], axis=1
                )
                both = jnp.dot(lhs_pair, rhs, preferred_element_type=jnp.float32)
                for k in range(2):
                    value = fold(both[:, k * LANES : (k + 1) * LANES], s_pair)
                    hid[base + row + k] = inside(row + k, value).astype(jnp.bfloat16)
            for row in range(low, high, 2):
                rows = [hid[base + r] for r in range(row - 1, row + 3)]
                rhs = jnp.concatenate(
                    [jnp.concatenate(rows[0:3], axis=0), jnp.concatenate(rows[1:4], axis=0)], axis=1
                )
                both = jnp.dot(lhs_mixed, rhs, preferred_element_type=jnp.float32)
                for k in range(2):
                    emit(row + k, fold(both[:, k * LANES : (k + 1) * LANES], s_mixed))

        for pair in range(2):

            def emit_one(row, branch, pair=pair):
                first = frame_row(row, pair)[:CH].astype(jnp.float32)
                one[row, pair * CH : (pair + 1) * CH, :] = inside(row, first + branch).astype(jnp.bfloat16)

            level(lambda row, pair=pair: frame_row(row, pair), 16 * pair, 2, 14, emit_one)

        def emit_two(row, branch):
            first = one[row, :CH, :].astype(jnp.float32)
            wide[pl.ds(row - HALO, CH, stride=ROWS), :] = first + branch

        level(lambda row: one[row], 32, HALO, HALO + ROWS, emit_two)
        out_r[...] = wide[...].reshape(CH, ROWS, LANES).astype(jnp.bfloat16)

    return pl.pallas_call(
        body,
        out_shape=jax.ShapeDtypeStruct((CH, ROWS, LANES), jnp.bfloat16),
        in_specs=[pl.BlockSpec(memory_space=pltpu.VMEM)] * 8,
        scratch_shapes=[
            pltpu.VMEM((48, CH, LANES), jnp.bfloat16),
            pltpu.VMEM((16, 2 * CH, LANES), jnp.bfloat16),
            pltpu.VMEM((CH * ROWS, LANES), jnp.float32),
        ],
        compiler_params=pltpu.CompilerParams(vmem_limit_bytes=16 << 20),
        name="merges",
    )(above, top, bottom, below, w_pair, w_mixed, slope_pair, slope_mixed)


def on_device(frames, w_pair, w_mixed, slope_pair, slope_mixed):
    count = lax.axis_size("frame")
    quarter = count // 4
    groups = [[a + quarter * b for b in range(4)] for a in range(quarter)]
    stack = lax.all_to_all(frames, "frame", 0, 0, axis_index_groups=groups, tiled=True)
    top, bottom = rows_first(stack)
    ends = lax.axis_size("row") - 1
    above = lax.ppermute(bottom, "row", [(i, i + 1) for i in range(ends)])
    below = lax.ppermute(top, "row", [(i + 1, i) for i in range(ends)])
    merged = merges(
        above,
        top,
        bottom,
        below,
        w_pair.reshape(3, 3 * CH, 2 * CH),
        w_mixed.reshape(3, 3 * CH, CH),
        slope_pair.reshape(1, CH),
        slope_mixed.reshape(1, CH),
    )
    return merged[None]


def solution(mesh):
    placed = (P("frame", None, "row", None), P(), P(), P(), P())
    return jax.shard_map(
        on_device,
        mesh=mesh,
        in_specs=placed,
        out_specs=P("frame", None, "row", None),
        check_vma=False,
    )
```

```python
import jax
import jax.numpy as jnp
from jax import lax
from jax.experimental import pallas as pl
from jax.experimental.pallas import tpu as pltpu
from jax.sharding import PartitionSpec as P


ROWS = 8
HALO = 4
CH = 64
LANES = 128
VMEM = pl.BlockSpec(memory_space=pltpu.VMEM)
SMALL = pltpu.CompilerParams(vmem_limit_bytes=8 << 20)


def array(*shape, dtype=jnp.bfloat16):
    return jax.ShapeDtypeStruct(shape, dtype)


def spread(frames):
    def body(src, own, one, two, three, held, wide, sems):
        at = lax.axis_index("frame") // (lax.axis_size("frame") // 4)
        outs = (own, one, two, three)
        order = (1, 3, 2, 0)

        def copy(k):
            return pltpu.make_async_copy(src.at[(at + k) % 4], held.at[k], sems.at[k])

        for k in order:
            copy(k).start()
        for k in order:
            copy(k).wait()
            wide[k] = held[k].astype(jnp.float32).reshape(CH * ROWS, LANES)
            for row in range(ROWS):
                outs[k][row] = wide[k, pl.ds(row, CH, stride=ROWS), :].astype(jnp.bfloat16)

    return pl.pallas_call(
        body,
        out_shape=(array(ROWS, CH, LANES),) * 4,
        in_specs=[pl.BlockSpec(memory_space=pltpu.HBM)],
        out_specs=(VMEM,) * 4,
        scratch_shapes=[
            pltpu.VMEM((4, CH, ROWS, LANES), jnp.bfloat16),
            pltpu.VMEM((4, CH * ROWS, LANES), jnp.float32),
            pltpu.SemaphoreType.DMA((4,)),
        ],
        compiler_params=SMALL,
        name="spread",
    )(frames)


def weights(w_pair, w_mixed, slope_pair, slope_mixed):
    def body(wp, wm, sp, sm, pair, mixed, cols):
        for ky in range(3):
            at = ky * 2 * CH
            pair[0, :, at : at + 2 * CH] = wp[ky]
            pair[1, :, at : at + 2 * CH] = jnp.concatenate([wp[ky][:, CH:], wp[ky][:, :CH]], axis=1)
        mixed[...] = jnp.concatenate([wm[0], wm[1], wm[2]], axis=1)
        square = lax.broadcasted_iota(jnp.int32, (CH, CH), 0) == lax.broadcasted_iota(jnp.int32, (CH, CH), 1)
        for k, slope in enumerate((sp, sm)):
            column = jnp.sum(jnp.where(square, slope[...], 0.0), axis=1, keepdims=True)
            cols[k] = jnp.broadcast_to(column, (CH, LANES))

    return pl.pallas_call(
        body,
        out_shape=(array(2, 3 * CH, 6 * CH), array(3 * CH, 3 * CH), array(2, CH, LANES, dtype=jnp.float32)),
        in_specs=[VMEM] * 4,
        out_specs=(VMEM,) * 3,
        compiler_params=SMALL,
        name="weights",
    )(w_pair.reshape(3, 3 * CH, 2 * CH), w_mixed.reshape(3, 3 * CH, CH), slope_pair.reshape(1, CH), slope_mixed.reshape(1, CH))


def edges(*frames):
    def body(*refs):
        top, bottom = refs[-2:]
        for k, frame in enumerate(refs[:-2]):
            top[:, k * CH : (k + 1) * CH, :] = frame[:HALO]
            bottom[:, k * CH : (k + 1) * CH, :] = frame[HALO:]

    half = array(HALO, len(frames) * CH, LANES)
    return pl.pallas_call(
        body,
        out_shape=(half, half),
        in_specs=[VMEM] * len(frames),
        out_specs=(VMEM,) * 2,
        compiler_params=SMALL,
        name="edges",
    )(*frames)


class Level:
    def __init__(self, pair, mixed, cols, swap, hid):
        lane = lax.broadcasted_iota(jnp.int32, (CH, LANES), 1)
        self.not_first = lane > 0
        self.not_last = lane < LANES - 1
        self.pair = pair[swap]
        self.mixed = mixed[...]
        self.cols = cols
        self.swap = swap
        self.hid = hid
        self.place = lax.axis_index("row")
        self.last = lax.axis_size("row") - 1

    def inside(self, row, value):
        if row < HALO:
            return jnp.where(self.place > 0, value, 0.0)
        if row >= HALO + ROWS:
            return jnp.where(self.place < self.last, value, 0.0)
        return value

    def fold(self, part, which):
        left = jnp.where(self.not_first, pltpu.roll(part[:CH], 1, 1), 0.0)
        right = jnp.where(self.not_last, pltpu.roll(part[2 * CH :], LANES - 1, 1), 0.0)
        total = part[CH : 2 * CH] + left + right
        return jnp.where(total >= 0, total, self.cols[which] * total)

    def product(self, lhs, rows):
        rhs = jnp.concatenate([jnp.concatenate(rows[0:3], axis=0), jnp.concatenate(rows[1:4], axis=0)], axis=1)
        return jnp.dot(lhs, rhs, preferred_element_type=jnp.float32)

    def run(self, one, two, low, high, emit):
        for row in range(low - 1, high + 1, 2):
            rows = [jnp.concatenate([one(r), two(r)], axis=0) for r in range(row - 1, row + 3)]
            both = self.product(self.pair, rows)
            for k in range(2):
                value = self.fold(both[:, k * LANES : (k + 1) * LANES], 0)
                self.hid[row + k] = self.inside(row + k, value).astype(jnp.bfloat16)
        for row in range(low, high, 2):
            both = self.product(self.mixed, [self.hid[r] for r in range(row - 1, row + 3)])
            for k in range(2):
                first = jnp.where(self.swap > 0, two(row + k).astype(jnp.float32), one(row + k).astype(jnp.float32))
                branch = self.fold(both[:, k * LANES : (k + 1) * LANES], 1)
                emit(row + k, self.inside(row + k, first + branch))


def rows_of(above, frame, below, slot):
    def load(row):
        if row < HALO:
            return above[row, slot * CH : (slot + 1) * CH, :]
        if row < HALO + ROWS:
            return frame[row - HALO]
        return below[row - HALO - ROWS, slot * CH : (slot + 1) * CH, :]

    return load


def position():
    return lax.axis_index("frame") // (lax.axis_size("frame") // 4)


def merge_near(above, before, after, below, tables):
    def body(above_r, before_r, after_r, below_r, pair, mixed, cols, out, hid):
        at = position()
        swap = jnp.where((at == 0) | (at == 3), 1, 0)
        level = Level(pair, mixed, cols, swap, hid)

        def emit(row, value):
            out[row - 2] = value.astype(jnp.bfloat16)

        level.run(rows_of(above_r, before_r, below_r, 1), rows_of(above_r, after_r, below_r, 2), 2, 14, emit)

    return pl.pallas_call(
        body,
        out_shape=array(12, CH, LANES),
        in_specs=[VMEM] * 7,
        out_specs=VMEM,
        scratch_shapes=[pltpu.VMEM((16, CH, LANES), jnp.bfloat16)],
        compiler_params=SMALL,
        name="merge_near",
    )(above, before, after, below, *tables)


def merge_rest(above, own, below, above_far, far, below_far, near, tables):
    def body(above_r, own_r, below_r, above_far_r, far_r, below_far_r, near_r, pair, mixed, cols, out, hid, hid_two, mine, wide):
        at = position()
        level = Level(pair, mixed, cols, jnp.where(at >= 2, 1, 0), hid)

        def emit(row, value):
            mine[row - 2] = value.astype(jnp.bfloat16)

        level.run(rows_of(above_r, own_r, below_r, 0), rows_of(above_far_r, far_r, below_far_r, 0), 2, 14, emit)
        top = Level(pair, mixed, cols, at % 2, hid_two)

        def emit_two(row, value):
            wide[pl.ds(row - HALO, CH, stride=ROWS), :] = value

        top.run(lambda row: mine[row - 2], lambda row: near_r[row - 2], HALO, HALO + ROWS, emit_two)
        out[...] = wide[...].reshape(CH, ROWS, LANES).astype(jnp.bfloat16)

    return pl.pallas_call(
        body,
        out_shape=array(CH, ROWS, LANES),
        in_specs=[VMEM] * 10,
        scratch_shapes=[
            pltpu.VMEM((16, CH, LANES), jnp.bfloat16),
            pltpu.VMEM((16, CH, LANES), jnp.bfloat16),
            pltpu.VMEM((12, CH, LANES), jnp.bfloat16),
            pltpu.VMEM((CH * ROWS, LANES), jnp.float32),
        ],
        compiler_params=SMALL,
        name="merge_rest",
    )(above, own, below, above_far, far, below_far, near, *tables)


def on_device(frames, w_pair, w_mixed, slope_pair, slope_mixed):
    count = lax.axis_size("frame")
    quarter = count // 4
    ends = lax.axis_size("row") - 1

    def turned(block, by):
        return lax.ppermute(block, "frame", [(i, (i + by * quarter) % count) for i in range(count)])

    def halos(top, bottom):
        above = lax.ppermute(bottom, "row", [(i, i + 1) for i in range(ends)])
        below = lax.ppermute(top, "row", [(i + 1, i) for i in range(ends)])
        return above, below

    own, one, two, three = spread(frames)
    before = turned(one, 1)
    after = turned(three, 3)
    far = turned(two, 2)
    tables = weights(w_pair, w_mixed, slope_pair, slope_mixed)
    near_edges = edges(own, before, after)
    above, below = halos(*near_edges)
    far_edges = edges(far)
    above_far, below_far = halos(*far_edges)
    near = merge_near(above, before, after, below, tables)
    merged = merge_rest(above, own, below, above_far, far, below_far, near, tables)
    return merged[None]


def solution(mesh):
    placed = (P("frame", None, "row", None), P(), P(), P(), P())
    return jax.shard_map(
        on_device,
        mesh=mesh,
        in_specs=placed,
        out_specs=P("frame", None, "row", None),
        check_vma=False,
    )
```

```python
import jax
import jax.numpy as jnp
from jax import lax
from jax.experimental import pallas as pl
from jax.experimental.pallas import tpu as pltpu
from jax.sharding import PartitionSpec as P


ROWS = 8
HALO = 4
CH = 64
LANES = 128
VMEM = pl.BlockSpec(memory_space=pltpu.VMEM)
SMALL = pltpu.CompilerParams(vmem_limit_bytes=8 << 20)


def array(*shape, dtype=jnp.bfloat16):
    return jax.ShapeDtypeStruct(shape, dtype)


def position():
    return lax.axis_index("frame") // (lax.axis_size("frame") // 4)


def spread(frames):
    def body(src, own, one, three, two, wide):
        at = position()
        for k, out in ((1, one), (3, three), (2, two), (0, own)):
            wide[k] = src[at ^ k].astype(jnp.float32).reshape(CH * ROWS, LANES)
            for row in range(ROWS):
                out[row] = wide[k, pl.ds(row, CH, stride=ROWS), :].astype(jnp.bfloat16)

    return pl.pallas_call(
        body,
        out_shape=(array(ROWS, CH, LANES),) * 4,
        in_specs=[VMEM],
        out_specs=(VMEM,) * 4,
        scratch_shapes=[pltpu.VMEM((4, CH * ROWS, LANES), jnp.float32)],
        compiler_params=SMALL,
        name="spread",
    )(frames)


def weights(w_pair, w_mixed, slope_pair, slope_mixed):
    def body(wp, wm, sp, sm, pair, mixed, cols):
        for ky in range(3):
            at = ky * 2 * CH
            pair[0, :, at : at + 2 * CH] = wp[ky]
            pair[1, :, at : at + 2 * CH] = jnp.concatenate([wp[ky][:, CH:], wp[ky][:, :CH]], axis=1)
        mixed[...] = jnp.concatenate([wm[0], wm[1], wm[2]], axis=1)
        square = lax.broadcasted_iota(jnp.int32, (CH, CH), 0) == lax.broadcasted_iota(jnp.int32, (CH, CH), 1)
        for k, slope in enumerate((sp, sm)):
            column = jnp.sum(jnp.where(square, slope[...], 0.0), axis=1, keepdims=True)
            cols[k] = jnp.broadcast_to(column, (CH, LANES))

    return pl.pallas_call(
        body,
        out_shape=(array(2, 3 * CH, 6 * CH), array(3 * CH, 3 * CH), array(2, CH, LANES, dtype=jnp.float32)),
        in_specs=[VMEM] * 4,
        out_specs=(VMEM,) * 3,
        compiler_params=SMALL,
        name="weights",
    )(w_pair.reshape(3, 3 * CH, 2 * CH), w_mixed.reshape(3, 3 * CH, CH), slope_pair.reshape(1, CH), slope_mixed.reshape(1, CH))


def edges(*frames):
    def body(*refs):
        near_side, far_side = refs[-2:]
        odd = lax.axis_index("row") % 2
        for k, frame in enumerate(refs[:-2]):
            near_side[:, k * CH : (k + 1) * CH, :] = frame[pl.ds(HALO - HALO * odd, HALO)]
            far_side[:, k * CH : (k + 1) * CH, :] = frame[pl.ds(HALO * odd, HALO)]

    half = array(HALO, len(frames) * CH, LANES)
    return pl.pallas_call(
        body,
        out_shape=(half, half),
        in_specs=[VMEM] * len(frames),
        out_specs=(VMEM,) * 2,
        compiler_params=SMALL,
        name="edges",
    )(*frames)


def fill(stack, slot, near_side, frame, far_side, part):
    odd = lax.axis_index("row") % 2
    to = slice(slot * CH, (slot + 1) * CH)
    of = slice(part * CH, (part + 1) * CH)
    stack[HALO : HALO + ROWS, to, :] = frame[...]
    stack[pl.ds((HALO + ROWS) * (1 - odd), HALO), to, :] = near_side[:, of, :]
    stack[pl.ds((HALO + ROWS) * odd, HALO), to, :] = far_side[:, of, :]


class Level:
    def __init__(self, pair, mixed, cols, swap, hid):
        lane = lax.broadcasted_iota(jnp.int32, (CH, LANES), 1)
        self.not_first = lane > 0
        self.not_last = lane < LANES - 1
        self.pair = pair[swap]
        self.mixed = mixed[...]
        self.cols = cols
        self.swap = swap
        self.hid = hid
        self.place = lax.axis_index("row")
        self.last = lax.axis_size("row") - 1

    def inside(self, row, value):
        if row < HALO:
            return jnp.where(self.place > 0, value, 0.0)
        if row >= HALO + ROWS:
            return jnp.where(self.place < self.last, value, 0.0)
        return value

    def fold(self, part, which):
        left = jnp.where(self.not_first, pltpu.roll(part[:CH], 1, 1), 0.0)
        right = jnp.where(self.not_last, pltpu.roll(part[2 * CH :], LANES - 1, 1), 0.0)
        total = part[CH : 2 * CH] + left + right
        return jnp.where(total >= 0, total, self.cols[which] * total)

    def product(self, lhs, stack, row, depth):
        rhs = jnp.concatenate([stack[r - 1 : r + 2].reshape(3 * depth, LANES) for r in (row, row + 1)], axis=1)
        return jnp.dot(lhs, rhs, preferred_element_type=jnp.float32)

    def run(self, stack, shift, low, high, emit):
        for row in range(low - 1, high + 1, 2):
            both = self.product(self.pair, stack, row - shift, 2 * CH)
            for k in range(2):
                value = self.fold(both[:, k * LANES : (k + 1) * LANES], 0)
                self.hid[row + k] = self.inside(row + k, value).astype(jnp.bfloat16)
        for row in range(low, high, 2):
            both = self.product(self.mixed, self.hid, row, CH)
            for k in range(2):
                first = stack[row + k - shift, pl.ds(self.swap * CH, CH), :].astype(jnp.float32)
                branch = self.fold(both[:, k * LANES : (k + 1) * LANES], 1)
                emit(row + k, self.inside(row + k, first + branch))


def merge_near(near_side, one, three, far_side, tables):
    def body(near_r, one_r, three_r, far_r, pair, mixed, cols, out, stack, hid):
        fill(stack, 0, near_r, one_r, far_r, 1)
        fill(stack, 1, near_r, three_r, far_r, 2)
        level = Level(pair, mixed, cols, position() // 2, hid)

        def emit(row, value):
            out[row - 2] = value.astype(jnp.bfloat16)

        level.run(stack, 0, 2, 14, emit)

    return pl.pallas_call(
        body,
        out_shape=array(12, CH, LANES),
        in_specs=[VMEM] * 7,
        out_specs=VMEM,
        scratch_shapes=[
            pltpu.VMEM((16, 2 * CH, LANES), jnp.bfloat16),
            pltpu.VMEM((16, CH, LANES), jnp.bfloat16),
        ],
        compiler_params=SMALL,
        name="merge_near",
    )(near_side, one, three, far_side, *tables)


def merge_rest(near_side, own, far_side, near_side_two, two, far_side_two, near, tables):
    def body(near_r, own_r, far_r, near_two_r, two_r, far_two_r, near_level, pair, mixed, cols, out, stack, ones, hid, hid_two, wide):
        fill(stack, 0, near_r, own_r, far_r, 0)
        fill(stack, 1, near_two_r, two_r, far_two_r, 0)
        ones[:, CH:, :] = near_level[...]
        level = Level(pair, mixed, cols, position() // 2, hid)

        def emit(row, value):
            ones[row - 2, :CH, :] = value.astype(jnp.bfloat16)

        level.run(stack, 0, 2, 14, emit)
        top = Level(pair, mixed, cols, position() % 2, hid_two)

        def emit_two(row, value):
            wide[pl.ds(row - HALO, CH, stride=ROWS), :] = value

        top.run(ones, 2, HALO, HALO + ROWS, emit_two)
        out[...] = wide[...].reshape(CH, ROWS, LANES).astype(jnp.bfloat16)

    return pl.pallas_call(
        body,
        out_shape=array(CH, ROWS, LANES),
        in_specs=[VMEM] * 10,
        scratch_shapes=[
            pltpu.VMEM((16, 2 * CH, LANES), jnp.bfloat16),
            pltpu.VMEM((12, 2 * CH, LANES), jnp.bfloat16),
            pltpu.VMEM((16, CH, LANES), jnp.bfloat16),
            pltpu.VMEM((16, CH, LANES), jnp.bfloat16),
            pltpu.VMEM((CH * ROWS, LANES), jnp.float32),
        ],
        compiler_params=SMALL,
        name="merge_rest",
    )(near_side, own, far_side, near_side_two, two, far_side_two, near, *tables)


def on_device(frames, w_pair, w_mixed, slope_pair, slope_mixed):
    count = lax.axis_size("frame")
    quarter = count // 4
    rows = lax.axis_size("row")

    def swapped(block, mask):
        return lax.ppermute(block, "frame", [(i, i ^ (mask * quarter)) for i in range(count)])

    def on_chip(block):
        return lax.ppermute(block, "row", [(i, i ^ 1) for i in range(rows)])

    def off_chip(block):
        return lax.ppermute(block, "row", [(i, ((i + 1) ^ 1) - 1) for i in range(1, rows - 1)])

    own, one, three, two = spread(frames)
    one = swapped(one, 1)
    three = swapped(three, 3)
    two = swapped(two, 2)
    tables = weights(w_pair, w_mixed, slope_pair, slope_mixed)
    near_side, far_side = edges(own, one, three)
    far_side = off_chip(far_side)
    near_side = on_chip(near_side)
    near_side_two, far_side_two = edges(two)
    far_side_two = off_chip(far_side_two)
    near_side_two = on_chip(near_side_two)
    near = merge_near(near_side, one, three, far_side, tables)
    merged = merge_rest(near_side, own, far_side, near_side_two, two, far_side_two, near, tables)
    return merged[None]


def solution(mesh):
    placed = (P("frame", None, "row", None), P(), P(), P(), P())
    return jax.shard_map(
        on_device,
        mesh=mesh,
        in_specs=placed,
        out_specs=P("frame", None, "row", None),
        check_vma=False,
    )
```

```python
import jax
import jax.numpy as jnp
from jax import lax
from jax.experimental import pallas as pl
from jax.experimental.pallas import tpu as pltpu
from jax.sharding import PartitionSpec as P


ROWS = 8
HALO = 4
CH = 64
LANES = 128
VMEM = pl.BlockSpec(memory_space=pltpu.VMEM)
SMALL = pltpu.CompilerParams(vmem_limit_bytes=8 << 20)


def array(*shape, dtype=jnp.bfloat16):
    return jax.ShapeDtypeStruct(shape, dtype)


def position():
    return lax.axis_index("frame") // (lax.axis_size("frame") // 4)


def spread(frames):
    def body(src, own, one, three, two, wide):
        at = position()
        for k, out in ((1, one), (3, three), (2, two), (0, own)):
            wide[k] = src[at ^ k].astype(jnp.float32).reshape(CH * ROWS, LANES)
            for row in range(ROWS):
                out[row] = wide[k, pl.ds(row, CH, stride=ROWS), :].astype(jnp.bfloat16)

    return pl.pallas_call(
        body,
        out_shape=(array(ROWS, CH, LANES),) * 4,
        in_specs=[VMEM],
        out_specs=(VMEM,) * 4,
        scratch_shapes=[pltpu.VMEM((4, CH * ROWS, LANES), jnp.float32)],
        compiler_params=SMALL,
        name="spread",
    )(frames)


def weights(w_pair, w_mixed, slope_pair, slope_mixed):
    def body(wp, wm, sp, sm, pair, mixed, cols):
        for ky in range(3):
            at = ky * 2 * CH
            pair[0, :, at : at + 2 * CH] = wp[ky]
            pair[1, :, at : at + 2 * CH] = jnp.concatenate([wp[ky][:, CH:], wp[ky][:, :CH]], axis=1)
        mixed[...] = jnp.concatenate([wm[0], wm[1], wm[2]], axis=1)
        square = lax.broadcasted_iota(jnp.int32, (CH, CH), 0) == lax.broadcasted_iota(jnp.int32, (CH, CH), 1)
        for k, slope in enumerate((sp, sm)):
            column = jnp.sum(jnp.where(square, slope[...], 0.0), axis=1, keepdims=True)
            cols[k] = jnp.broadcast_to(column, (CH, LANES))

    return pl.pallas_call(
        body,
        out_shape=(array(2, 3 * CH, 6 * CH), array(3 * CH, 3 * CH), array(2, CH, LANES, dtype=jnp.float32)),
        in_specs=[VMEM] * 4,
        out_specs=(VMEM,) * 3,
        compiler_params=SMALL,
        name="weights",
    )(w_pair.reshape(3, 3 * CH, 2 * CH), w_mixed.reshape(3, 3 * CH, CH), slope_pair.reshape(1, CH), slope_mixed.reshape(1, CH))


def edges(*frames):
    def body(*refs):
        near_side, far_side = refs[-2:]
        odd = lax.axis_index("row") % 2
        for k, frame in enumerate(refs[:-2]):
            near_side[:, k * CH : (k + 1) * CH, :] = frame[pl.ds(HALO - HALO * odd, HALO)]
            far_side[:, k * CH : (k + 1) * CH, :] = frame[pl.ds(HALO * odd, HALO)]

    half = array(HALO, len(frames) * CH, LANES)
    return pl.pallas_call(
        body,
        out_shape=(half, half),
        in_specs=[VMEM] * len(frames),
        out_specs=(VMEM,) * 2,
        compiler_params=SMALL,
        name="edges",
    )(*frames)


def fill(stack, slot, near_side, frame, far_side, part):
    odd = lax.axis_index("row") % 2
    to = slice(slot * CH, (slot + 1) * CH)
    of = slice(part * CH, (part + 1) * CH)
    stack[HALO : HALO + ROWS, to, :] = frame[...]
    stack[pl.ds((HALO + ROWS) * (1 - odd), HALO), to, :] = near_side[:, of, :]
    stack[pl.ds((HALO + ROWS) * odd, HALO), to, :] = far_side[:, of, :]


class Level:
    def __init__(self, pair, mixed, cols, swap, hid):
        lane = lax.broadcasted_iota(jnp.int32, (CH, LANES), 1)
        self.not_first = lane > 0
        self.not_last = lane < LANES - 1
        self.pair = pair[swap]
        self.mixed = mixed[...]
        self.cols = cols
        self.swap = swap
        self.hid = hid
        self.place = lax.axis_index("row")
        self.last = lax.axis_size("row") - 1

    def inside(self, row, value):
        if row < HALO:
            return jnp.where(self.place > 0, value, 0.0)
        if row >= HALO + ROWS:
            return jnp.where(self.place < self.last, value, 0.0)
        return value

    def fold(self, part, which):
        left = jnp.where(self.not_first, pltpu.roll(part[:CH], 1, 1), 0.0)
        right = jnp.where(self.not_last, pltpu.roll(part[2 * CH :], LANES - 1, 1), 0.0)
        total = part[CH : 2 * CH] + left + right
        return jnp.where(total >= 0, total, self.cols[which] * total)

    def product(self, lhs, stack, row, depth):
        rhs = jnp.concatenate([stack[r - 1 : r + 2].reshape(3 * depth, LANES) for r in (row, row + 1)], axis=1)
        return jnp.dot(lhs, rhs, preferred_element_type=jnp.float32)

    def run(self, stack, shift, low, high, emit):
        for row in range(low - 1, high + 1, 2):
            both = self.product(self.pair, stack, row - shift, 2 * CH)
            for k in range(2):
                value = self.fold(both[:, k * LANES : (k + 1) * LANES], 0)
                self.hid[row + k] = self.inside(row + k, value).astype(jnp.bfloat16)
        for row in range(low, high, 2):
            both = self.product(self.mixed, self.hid, row, CH)
            for k in range(2):
                first = stack[row + k - shift, pl.ds(self.swap * CH, CH), :].astype(jnp.float32)
                branch = self.fold(both[:, k * LANES : (k + 1) * LANES], 1)
                emit(row + k, self.inside(row + k, first + branch))


def merges(sides_early, sides_late, own, one, two, three, tables):
    def body(near_a, far_a, near_b, far_b, own_r, one_r, two_r, three_r, pair, mixed, cols, out, stack, other, ones, hid, wide):
        fill(other, 0, near_a, one_r, far_a, 1)
        fill(other, 1, near_b, three_r, far_b, 1)
        fill(stack, 0, near_a, own_r, far_a, 0)
        fill(stack, 1, near_b, two_r, far_b, 0)
        at = position()
        for k, rows in ((1, other), (0, stack)):

            def emit(row, value, k=k):
                ones[row - 2, k * CH : (k + 1) * CH, :] = value.astype(jnp.bfloat16)

            Level(pair, mixed, cols, at // 2, hid.at[k]).run(rows, 0, 2, 14, emit)

        def emit_two(row, value):
            wide[pl.ds(row - HALO, CH, stride=ROWS), :] = value

        Level(pair, mixed, cols, at % 2, hid.at[2]).run(ones, 2, HALO, HALO + ROWS, emit_two)
        out[...] = wide[...].reshape(CH, ROWS, LANES).astype(jnp.bfloat16)

    return pl.pallas_call(
        body,
        out_shape=array(CH, ROWS, LANES),
        in_specs=[VMEM] * 11,
        scratch_shapes=[
            pltpu.VMEM((16, 2 * CH, LANES), jnp.bfloat16),
            pltpu.VMEM((16, 2 * CH, LANES), jnp.bfloat16),
            pltpu.VMEM((12, 2 * CH, LANES), jnp.bfloat16),
            pltpu.VMEM((3, 16, CH, LANES), jnp.bfloat16),
            pltpu.VMEM((CH * ROWS, LANES), jnp.float32),
        ],
        compiler_params=SMALL,
        name="merges",
    )(*sides_early, *sides_late, own, one, two, three, *tables)


def on_device(frames, w_pair, w_mixed, slope_pair, slope_mixed):
    count = lax.axis_size("frame")
    quarter = count // 4
    rows = lax.axis_size("row")

    def swapped(block, mask):
        return lax.ppermute(block, "frame", [(i, i ^ (mask * quarter)) for i in range(count)])

    def on_chip(block):
        return lax.ppermute(block, "row", [(i, i ^ 1) for i in range(rows)])

    def off_chip(block):
        return lax.ppermute(block, "row", [(i, ((i + 1) ^ 1) - 1) for i in range(1, rows - 1)])

    own, one, three, two = spread(frames)
    one = swapped(one, 1)
    three = swapped(three, 3)
    two = swapped(two, 2)
    tables = weights(w_pair, w_mixed, slope_pair, slope_mixed)
    near_early, far_early = edges(own, one)
    far_early = off_chip(far_early)
    near_early = on_chip(near_early)
    near_late, far_late = edges(two, three)
    far_late = off_chip(far_late)
    near_late = on_chip(near_late)
    merged = merges((near_early, far_early), (near_late, far_late), own, one, two, three, tables)
    return merged[None]


def solution(mesh):
    placed = (P("frame", None, "row", None), P(), P(), P(), P())
    return jax.shard_map(
        on_device,
        mesh=mesh,
        in_specs=placed,
        out_specs=P("frame", None, "row", None),
        check_vma=False,
    )
```

```python
from functools import partial

import jax
import jax.numpy as jnp
from jax import lax
from jax.experimental import pallas as pl
from jax.experimental.pallas import tpu as pltpu
from jax.sharding import PartitionSpec as P


ROWS = 8
HALO = 4
CH = 64
LANES = 128
FRONT = 54400
VMEM = pl.BlockSpec(memory_space=pltpu.VMEM)
SMALL = pltpu.CompilerParams(vmem_limit_bytes=8 << 20)


def array(*shape, dtype=jnp.bfloat16):
    return jax.ShapeDtypeStruct(shape, dtype)


def position():
    return lax.axis_index("frame") // (lax.axis_size("frame") // 4)


def spread(frames, slope_pair, slope_mixed):
    def body(src, sp, sm, own, one, three, two, cols, held, wide, sems):
        at = position()
        order = ((2, two), (1, one), (3, three), (0, own))

        def copy(k):
            return pltpu.make_async_copy(src.at[at ^ k], held.at[k], sems.at[k])

        for k, _ in order:
            copy(k).start()
        square = lax.broadcasted_iota(jnp.int32, (CH, CH), 0) == lax.broadcasted_iota(jnp.int32, (CH, CH), 1)
        for k, slope in enumerate((sp, sm)):
            column = jnp.sum(jnp.where(square, slope[...], 0.0), axis=1, keepdims=True)
            cols[k] = jnp.broadcast_to(column, (CH, LANES))
        for k, out in order:
            copy(k).wait()
            wide[k] = held[k].astype(jnp.float32).reshape(CH * ROWS, LANES)
            for row in range(ROWS):
                out[row] = wide[k, pl.ds(row, CH, stride=ROWS), :].astype(jnp.bfloat16)

    return pl.pallas_call(
        body,
        out_shape=(array(ROWS, CH, LANES),) * 4 + (array(2, CH, LANES, dtype=jnp.float32),),
        in_specs=[pl.BlockSpec(memory_space=pl.ANY), VMEM, VMEM],
        out_specs=(VMEM,) * 5,
        scratch_shapes=[
            pltpu.VMEM((4, CH, ROWS, LANES), jnp.bfloat16),
            pltpu.VMEM((4, CH * ROWS, LANES), jnp.float32),
            pltpu.SemaphoreType.DMA((4,)),
        ],
        compiler_params=pltpu.CompilerParams(vmem_limit_bytes=FRONT << 10),
        name="spread",
    )(frames, slope_pair.reshape(1, CH), slope_mixed.reshape(1, CH))


def weights(w_pair, w_mixed):
    def body(wp, wm, pair, mixed):
        for ky in range(3):
            at = ky * 2 * CH
            pair[0, :, at : at + 2 * CH] = wp[ky]
            pair[1, :, at : at + 2 * CH] = jnp.concatenate([wp[ky][:, CH:], wp[ky][:, :CH]], axis=1)
        mixed[...] = jnp.concatenate([wm[0], wm[1], wm[2]], axis=1)

    return pl.pallas_call(
        body,
        out_shape=(array(2, 3 * CH, 6 * CH), array(3 * CH, 3 * CH)),
        in_specs=[VMEM] * 2,
        out_specs=(VMEM,) * 2,
        compiler_params=SMALL,
        name="weights",
    )(w_pair.reshape(3, 3 * CH, 2 * CH), w_mixed.reshape(3, 3 * CH, CH))


def edges(*frames):
    def body(*refs):
        near_side, far_side = refs[-2:]
        odd = lax.axis_index("row") % 2
        for k, frame in enumerate(refs[:-2]):
            near_side[:, k * CH : (k + 1) * CH, :] = frame[pl.ds(HALO - HALO * odd, HALO)]
            far_side[:, k * CH : (k + 1) * CH, :] = frame[pl.ds(HALO * odd, HALO)]

    half = array(HALO, len(frames) * CH, LANES)
    return pl.pallas_call(
        body,
        out_shape=(half, half),
        in_specs=[VMEM] * len(frames),
        out_specs=(VMEM,) * 2,
        compiler_params=SMALL,
        name="edges",
    )(*frames)


def fill(stack, slot, near_side, frame, far_side, part):
    odd = lax.axis_index("row") % 2
    to = slice(slot * CH, (slot + 1) * CH)
    of = slice(part * CH, (part + 1) * CH)
    stack[HALO : HALO + ROWS, to, :] = frame[...]
    stack[pl.ds((HALO + ROWS) * (1 - odd), HALO), to, :] = near_side[:, of, :]
    stack[pl.ds((HALO + ROWS) * odd, HALO), to, :] = far_side[:, of, :]


class Level:
    def __init__(self, pair, mixed, cols, swap, hid):
        lane = lax.broadcasted_iota(jnp.int32, (CH, LANES), 1)
        self.not_first = lane > 0
        self.not_last = lane < LANES - 1
        self.pair = pair[swap]
        self.mixed = mixed[...]
        self.cols = cols
        self.swap = swap
        self.hid = hid
        self.place = lax.axis_index("row")
        self.last = lax.axis_size("row") - 1

    def inside(self, row, value):
        if row < HALO:
            return jnp.where(self.place > 0, value, 0.0)
        if row >= HALO + ROWS:
            return jnp.where(self.place < self.last, value, 0.0)
        return value

    def fold(self, part, which):
        left = jnp.where(self.not_first, pltpu.roll(part[:CH], 1, 1), 0.0)
        right = jnp.where(self.not_last, pltpu.roll(part[2 * CH :], LANES - 1, 1), 0.0)
        total = part[CH : 2 * CH] + left + right
        return jnp.maximum(total, self.cols[which] * total)

    def product(self, lhs, stack, row, depth):
        rhs = jnp.concatenate([stack[r - 1 : r + 2].reshape(3 * depth, LANES) for r in (row, row + 1)], axis=1)
        return jnp.dot(lhs, rhs, preferred_element_type=jnp.float32)

    def steps(self, stack, shift, low, high, emit):
        def first_half(row):
            both = self.product(self.pair, stack, row - shift, 2 * CH)
            for k in range(2):
                value = self.fold(both[:, k * LANES : (k + 1) * LANES], 0)
                self.hid[row + k] = self.inside(row + k, value).astype(jnp.bfloat16)

        def second_half(row):
            both = self.product(self.mixed, self.hid, row, CH)
            for k in range(2):
                first = stack[row + k - shift, pl.ds(self.swap * CH, CH), :].astype(jnp.float32)
                branch = self.fold(both[:, k * LANES : (k + 1) * LANES], 1)
                emit(row + k, self.inside(row + k, first + branch))

        return (
            [partial(first_half, row) for row in range(low - 1, high + 1, 2)],
            [partial(second_half, row) for row in range(low, high, 2)],
        )


def run(*stages):
    for time in range(len(stages[0]) + 2 * len(stages)):
        for lag, stage in enumerate(stages):
            if 0 <= time - 2 * lag < len(stage):
                stage[time - 2 * lag]()


def merge_own(near_side, far_side, own, two, tables):
    def body(near_r, far_r, own_r, two_r, pair, mixed, cols, out, stack, hid):
        fill(stack, 0, near_r, own_r, far_r, 0)
        fill(stack, 1, near_r, two_r, far_r, 1)

        def emit(row, value):
            out[row - 2] = value.astype(jnp.bfloat16)

        run(*Level(pair, mixed, cols, position() // 2, hid).steps(stack, 0, 2, 14, emit))

    return pl.pallas_call(
        body,
        out_shape=array(12, CH, LANES),
        in_specs=[VMEM] * 7,
        out_specs=VMEM,
        scratch_shapes=[
            pltpu.VMEM((16, 2 * CH, LANES), jnp.bfloat16),
            pltpu.VMEM((16, CH, LANES), jnp.bfloat16),
        ],
        compiler_params=SMALL,
        name="merge_own",
    )(near_side, far_side, own, two, *tables)


def merge_rest(near_side, far_side, one, three, mine, tables):
    def body(near_r, far_r, one_r, three_r, mine_r, pair, mixed, cols, out, stack, ones, hid, hid_two, wide):
        fill(stack, 0, near_r, one_r, far_r, 0)
        fill(stack, 1, near_r, three_r, far_r, 1)
        ones[:, :CH, :] = mine_r[...]
        at = position()

        def emit(row, value):
            ones[row - 2, CH:, :] = value.astype(jnp.bfloat16)

        def emit_two(row, value):
            wide[pl.ds(row - HALO, CH, stride=ROWS), :] = value

        run(
            *Level(pair, mixed, cols, at // 2, hid).steps(stack, 0, 2, 14, emit),
            *Level(pair, mixed, cols, at % 2, hid_two).steps(ones, 2, HALO, HALO + ROWS, emit_two),
        )
        out[...] = wide[...].reshape(CH, ROWS, LANES).astype(jnp.bfloat16)

    return pl.pallas_call(
        body,
        out_shape=array(CH, ROWS, LANES),
        in_specs=[VMEM] * 8,
        scratch_shapes=[
            pltpu.VMEM((16, 2 * CH, LANES), jnp.bfloat16),
            pltpu.VMEM((12, 2 * CH, LANES), jnp.bfloat16),
            pltpu.VMEM((16, CH, LANES), jnp.bfloat16),
            pltpu.VMEM((16, CH, LANES), jnp.bfloat16),
            pltpu.VMEM((CH * ROWS, LANES), jnp.float32),
        ],
        compiler_params=SMALL,
        name="merge_rest",
    )(near_side, far_side, one, three, mine, *tables)


def on_device(frames, w_pair, w_mixed, slope_pair, slope_mixed):
    count = lax.axis_size("frame")
    quarter = count // 4
    rows = lax.axis_size("row")

    def swapped(block, mask):
        return lax.ppermute(block, "frame", [(i, i ^ (mask * quarter)) for i in range(count)])

    def on_chip(block):
        return lax.ppermute(block, "row", [(i, i ^ 1) for i in range(rows)])

    def off_chip(block):
        return lax.ppermute(block, "row", [(i, ((i + 1) ^ 1) - 1) for i in range(1, rows - 1)])

    own, one, three, two, cols = spread(frames, slope_pair, slope_mixed)
    one = swapped(one, 1)
    three = swapped(three, 3)
    two = swapped(two, 2)
    tables = (*weights(w_pair, w_mixed), cols)
    near_early, far_early = edges(own, two)
    far_early = off_chip(far_early)
    near_early = on_chip(near_early)
    near_late, far_late = edges(one, three)
    far_late = off_chip(far_late)
    near_late = on_chip(near_late)
    mine = merge_own(near_early, far_early, own, two, tables)
    merged = merge_rest(near_late, far_late, one, three, mine, tables)
    return merged[None]


def solution(mesh):
    placed = (P("frame", None, "row", None), P(), P(), P(), P())
    return jax.shard_map(
        on_device,
        mesh=mesh,
        in_specs=placed,
        out_specs=P("frame", None, "row", None),
        check_vma=False,
    )
```

```python
import jax
import jax.numpy as jnp
from jax import lax
from jax.experimental import pallas as pl
from jax.experimental.pallas import tpu as pltpu
from jax.sharding import PartitionSpec as P


ROWS = 8
HALO = 4
CH = 64
LANES = 128
VMEM = pl.BlockSpec(memory_space=pltpu.VMEM)
SMALL = pltpu.CompilerParams(vmem_limit_bytes=8 << 20)


def array(*shape, dtype=jnp.bfloat16):
    return jax.ShapeDtypeStruct(shape, dtype)


def position():
    return lax.axis_index("frame") // (lax.axis_size("frame") // 4)


def spread(frames):
    def body(src, own, one, three, two, wide):
        at = position()
        for k, out in ((2, two), (1, one), (3, three), (0, own)):
            wide[k] = src[at ^ k].astype(jnp.float32).reshape(CH * ROWS, LANES)
            for row in range(ROWS):
                out[row] = wide[k, pl.ds(row, CH, stride=ROWS), :].astype(jnp.bfloat16)

    return pl.pallas_call(
        body,
        out_shape=(array(ROWS, CH, LANES),) * 4,
        in_specs=[VMEM],
        out_specs=(VMEM,) * 4,
        scratch_shapes=[pltpu.VMEM((4, CH * ROWS, LANES), jnp.float32)],
        compiler_params=SMALL,
        name="spread",
    )(frames)


def weights(w_pair, w_mixed, slope_pair, slope_mixed):
    def body(wp, wm, sp, sm, pair, mixed, cols):
        for ky in range(3):
            at = ky * 2 * CH
            pair[0, :, at : at + 2 * CH] = wp[ky]
            pair[1, :, at : at + 2 * CH] = jnp.concatenate([wp[ky][:, CH:], wp[ky][:, :CH]], axis=1)
        mixed[...] = jnp.concatenate([wm[0], wm[1], wm[2]], axis=1)
        square = lax.broadcasted_iota(jnp.int32, (CH, CH), 0) == lax.broadcasted_iota(jnp.int32, (CH, CH), 1)
        for k, slope in enumerate((sp, sm)):
            column = jnp.sum(jnp.where(square, slope[...], 0.0), axis=1, keepdims=True)
            cols[k] = jnp.broadcast_to(column, (CH, LANES))

    return pl.pallas_call(
        body,
        out_shape=(array(2, 3 * CH, 6 * CH), array(3 * CH, 3 * CH), array(2, CH, LANES, dtype=jnp.float32)),
        in_specs=[VMEM] * 4,
        out_specs=(VMEM,) * 3,
        compiler_params=SMALL,
        name="weights",
    )(w_pair.reshape(3, 3 * CH, 2 * CH), w_mixed.reshape(3, 3 * CH, CH), slope_pair.reshape(1, CH), slope_mixed.reshape(1, CH))


def edges(*frames):
    def body(*refs):
        near_side, far_side = refs[-2:]
        odd = lax.axis_index("row") % 2
        for k, frame in enumerate(refs[:-2]):
            near_side[:, k * CH : (k + 1) * CH, :] = frame[pl.ds(HALO - HALO * odd, HALO)]
            far_side[:, k * CH : (k + 1) * CH, :] = frame[pl.ds(HALO * odd, HALO)]

    half = array(HALO, len(frames) * CH, LANES)
    return pl.pallas_call(
        body,
        out_shape=(half, half),
        in_specs=[VMEM] * len(frames),
        out_specs=(VMEM,) * 2,
        compiler_params=SMALL,
        name="edges",
    )(*frames)


def fill(stack, slot, near_side, frame, far_side, part):
    odd = lax.axis_index("row") % 2
    to = slice(slot * CH, (slot + 1) * CH)
    of = slice(part * CH, (part + 1) * CH)
    stack[HALO : HALO + ROWS, to, :] = frame[...]
    stack[pl.ds((HALO + ROWS) * (1 - odd), HALO), to, :] = near_side[:, of, :]
    stack[pl.ds((HALO + ROWS) * odd, HALO), to, :] = far_side[:, of, :]


class Level:
    def __init__(self, pair, mixed, cols, swap, hid):
        lane = lax.broadcasted_iota(jnp.int32, (CH, LANES), 1)
        self.not_first = lane > 0
        self.not_last = lane < LANES - 1
        self.pair = pair[swap]
        self.mixed = mixed[...]
        self.cols = cols
        self.swap = swap
        self.hid = hid
        self.place = lax.axis_index("row")
        self.last = lax.axis_size("row") - 1

    def inside(self, row, value):
        if row < HALO:
            return jnp.where(self.place > 0, value, 0.0)
        if row >= HALO + ROWS:
            return jnp.where(self.place < self.last, value, 0.0)
        return value

    def fold(self, part, which):
        left = jnp.where(self.not_first, pltpu.roll(part[:CH], 1, 1), 0.0)
        right = jnp.where(self.not_last, pltpu.roll(part[2 * CH :], LANES - 1, 1), 0.0)
        total = part[CH : 2 * CH] + left + right
        return jnp.maximum(total, self.cols[which] * total)

    def product(self, lhs, stack, row, depth):
        rhs = jnp.concatenate([stack[r - 1 : r + 2].reshape(3 * depth, LANES) for r in (row, row + 1)], axis=1)
        return jnp.dot(lhs, rhs, preferred_element_type=jnp.float32)

    def run(self, stack, shift, low, high, emit):
        for row in range(low - 1, high + 1, 2):
            both = self.product(self.pair, stack, row - shift, 2 * CH)
            for k in range(2):
                value = self.fold(both[:, k * LANES : (k + 1) * LANES], 0)
                self.hid[row + k] = self.inside(row + k, value).astype(jnp.bfloat16)
        for row in range(low, high, 2):
            both = self.product(self.mixed, self.hid, row, CH)
            for k in range(2):
                first = stack[row + k - shift, pl.ds(self.swap * CH, CH), :].astype(jnp.float32)
                branch = self.fold(both[:, k * LANES : (k + 1) * LANES], 1)
                emit(row + k, self.inside(row + k, first + branch))


def merge_own(near_side, far_side, own, two, tables):
    def body(near_r, far_r, own_r, two_r, pair, mixed, cols, out, stack, hid):
        fill(stack, 0, near_r, own_r, far_r, 0)
        fill(stack, 1, near_r, two_r, far_r, 1)

        def emit(row, value):
            out[row - 2] = value.astype(jnp.bfloat16)

        Level(pair, mixed, cols, position() // 2, hid).run(stack, 0, 2, 14, emit)

    return pl.pallas_call(
        body,
        out_shape=array(12, CH, LANES),
        in_specs=[VMEM] * 7,
        out_specs=VMEM,
        scratch_shapes=[
            pltpu.VMEM((16, 2 * CH, LANES), jnp.bfloat16),
            pltpu.VMEM((16, CH, LANES), jnp.bfloat16),
        ],
        compiler_params=SMALL,
        name="merge_own",
    )(near_side, far_side, own, two, *tables)


def merge_rest(near_side, far_side, one, three, mine, tables):
    def body(near_r, far_r, one_r, three_r, mine_r, pair, mixed, cols, out, stack, ones, hid, hid_two, wide):
        fill(stack, 0, near_r, one_r, far_r, 0)
        fill(stack, 1, near_r, three_r, far_r, 1)
        ones[:, :CH, :] = mine_r[...]
        at = position()

        def emit(row, value):
            ones[row - 2, CH:, :] = value.astype(jnp.bfloat16)

        Level(pair, mixed, cols, at // 2, hid).run(stack, 0, 2, 14, emit)

        def emit_two(row, value):
            wide[pl.ds(row - HALO, CH, stride=ROWS), :] = value

        Level(pair, mixed, cols, at % 2, hid_two).run(ones, 2, HALO, HALO + ROWS, emit_two)
        out[...] = wide[...].reshape(CH, ROWS, LANES).astype(jnp.bfloat16)

    return pl.pallas_call(
        body,
        out_shape=array(CH, ROWS, LANES),
        in_specs=[VMEM] * 8,
        scratch_shapes=[
            pltpu.VMEM((16, 2 * CH, LANES), jnp.bfloat16),
            pltpu.VMEM((12, 2 * CH, LANES), jnp.bfloat16),
            pltpu.VMEM((16, CH, LANES), jnp.bfloat16),
            pltpu.VMEM((16, CH, LANES), jnp.bfloat16),
            pltpu.VMEM((CH * ROWS, LANES), jnp.float32),
        ],
        compiler_params=SMALL,
        name="merge_rest",
    )(near_side, far_side, one, three, mine, *tables)


def on_device(frames, w_pair, w_mixed, slope_pair, slope_mixed):
    count = lax.axis_size("frame")
    quarter = count // 4
    rows = lax.axis_size("row")

    def swapped(block, mask):
        return lax.ppermute(block, "frame", [(i, i ^ (mask * quarter)) for i in range(count)])

    def on_chip(block):
        return lax.ppermute(block, "row", [(i, i ^ 1) for i in range(rows)])

    def off_chip(block):
        return lax.ppermute(block, "row", [(i, ((i + 1) ^ 1) - 1) for i in range(1, rows - 1)])

    own, one, three, two = spread(frames)
    one = swapped(one, 1)
    three = swapped(three, 3)
    two = swapped(two, 2)
    tables = weights(w_pair, w_mixed, slope_pair, slope_mixed)
    near_early, far_early = edges(own, two)
    far_early = off_chip(far_early)
    near_early = on_chip(near_early)
    near_late, far_late = edges(one, three)
    far_late = off_chip(far_late)
    near_late = on_chip(near_late)
    mine = merge_own(near_early, far_early, own, two, tables)
    merged = merge_rest(near_late, far_late, one, three, mine, tables)
    return merged[None]


def solution(mesh):
    placed = (P("frame", None, "row", None), P(), P(), P(), P())
    return jax.shard_map(
        on_device,
        mesh=mesh,
        in_specs=placed,
        out_specs=P("frame", None, "row", None),
        check_vma=False,
    )
```

```python
import jax
import jax.numpy as jnp
from jax import lax
from jax.experimental import pallas as pl
from jax.experimental.pallas import tpu as pltpu
from jax.sharding import PartitionSpec as P


ROWS = 8
HALO = 4
CH = 64
LANES = 128
VMEM = pl.BlockSpec(memory_space=pltpu.VMEM)
SMALL = pltpu.CompilerParams(vmem_limit_bytes=8 << 20)


def array(*shape, dtype=jnp.bfloat16):
    return jax.ShapeDtypeStruct(shape, dtype)


def position():
    return lax.axis_index("frame") // (lax.axis_size("frame") // 4)


def odd_row():
    return lax.axis_index("row") % 2


def spread(frames):
    def body(src, own, one, three, two, wide):
        at = position()
        turn = 7 - 7 * odd_row()
        sign = 2 * odd_row() - 1
        for k, out in ((2, two), (1, one), (3, three), (0, own)):
            wide[k] = src[at ^ k].astype(jnp.float32).reshape(CH * ROWS, LANES)
            for row in range(ROWS):
                out[turn + sign * row] = wide[k, pl.ds(row, CH, stride=ROWS), :].astype(jnp.bfloat16)

    return pl.pallas_call(
        body,
        out_shape=(array(ROWS, CH, LANES),) * 4,
        in_specs=[VMEM],
        out_specs=(VMEM,) * 4,
        scratch_shapes=[pltpu.VMEM((4, CH * ROWS, LANES), jnp.float32)],
        compiler_params=SMALL,
        name="spread",
    )(frames)


def weights(w_pair, w_mixed, slope_pair, slope_mixed):
    def body(wp, wm, sp, sm, pair, mixed, cols):
        top = 2 - 2 * odd_row()
        taps = (top, 1, 2 - top)
        for ky in range(3):
            at = ky * 2 * CH
            tap = wp[taps[ky]]
            pair[0, :, at : at + 2 * CH] = tap
            pair[1, :, at : at + 2 * CH] = jnp.concatenate([tap[:, CH:], tap[:, :CH]], axis=1)
        mixed[...] = jnp.concatenate([wm[taps[0]], wm[1], wm[taps[2]]], axis=1)
        square = lax.broadcasted_iota(jnp.int32, (CH, CH), 0) == lax.broadcasted_iota(jnp.int32, (CH, CH), 1)
        for k, slope in enumerate((sp, sm)):
            column = jnp.sum(jnp.where(square, slope[...], 0.0), axis=1, keepdims=True)
            cols[k] = jnp.broadcast_to(column, (CH, LANES))

    return pl.pallas_call(
        body,
        out_shape=(array(2, 3 * CH, 6 * CH), array(3 * CH, 3 * CH), array(2, CH, LANES, dtype=jnp.float32)),
        in_specs=[VMEM] * 4,
        out_specs=(VMEM,) * 3,
        compiler_params=SMALL,
        name="weights",
    )(w_pair.reshape(3, 3 * CH, 2 * CH), w_mixed.reshape(3, 3 * CH, CH), slope_pair.reshape(1, CH), slope_mixed.reshape(1, CH))


def edges(*frames):
    def body(*refs):
        near_side, far_side = refs[-2:]
        for k, frame in enumerate(refs[:-2]):
            for row in range(HALO):
                near_side[row, k * CH : (k + 1) * CH, :] = frame[HALO - 1 - row]
                far_side[row, k * CH : (k + 1) * CH, :] = frame[ROWS - 1 - row]

    half = array(HALO, len(frames) * CH, LANES)
    return pl.pallas_call(
        body,
        out_shape=(half, half),
        in_specs=[VMEM] * len(frames),
        out_specs=(VMEM,) * 2,
        compiler_params=SMALL,
        name="edges",
    )(*frames)


def fill(stack, slot, source, at, part=0):
    to = slice(slot * CH, (slot + 1) * CH)
    stack[at : at + source.shape[0], to, :] = source[:, part * CH : (part + 1) * CH, :]


class Level:
    def __init__(self, pair, mixed, cols, swap, hid):
        lane = lax.broadcasted_iota(jnp.int32, (CH, LANES), 1)
        self.not_first = lane > 0
        self.not_last = lane < LANES - 1
        self.pair = pair[swap]
        self.mixed = mixed[...]
        self.cols = cols
        self.swap = swap
        self.hid = hid
        place = lax.axis_index("row")
        self.edge = (place == 0) | (place == lax.axis_size("row") - 1)

    def inside(self, row, value):
        return jnp.where(self.edge, 0.0, value) if row >= HALO + ROWS else value

    def fold(self, part, which):
        left = jnp.where(self.not_first, pltpu.roll(part[:CH], 1, 1), 0.0)
        right = jnp.where(self.not_last, pltpu.roll(part[2 * CH :], LANES - 1, 1), 0.0)
        total = part[CH : 2 * CH] + left + right
        return jnp.maximum(total, self.cols[which] * total)

    def product(self, lhs, stack, row, depth):
        rhs = jnp.concatenate([stack[r - 1 : r + 2].reshape(3 * depth, LANES) for r in (row, row + 1)], axis=1)
        return jnp.dot(lhs, rhs, preferred_element_type=jnp.float32)

    def first(self, stack, shift, low, high):
        for row in range(low, high, 2):
            both = self.product(self.pair, stack, row - shift, 2 * CH)
            for k in range(2):
                value = self.fold(both[:, k * LANES : (k + 1) * LANES], 0)
                self.hid[row + k] = self.inside(row + k, value).astype(jnp.bfloat16)

    def second(self, stack, shift, low, high, emit):
        for row in range(low, high, 2):
            both = self.product(self.mixed, self.hid, row, CH)
            for k in range(2):
                start = stack[row + k - shift, pl.ds(self.swap * CH, CH), :].astype(jnp.float32)
                branch = self.fold(both[:, k * LANES : (k + 1) * LANES], 1)
                emit(row + k, self.inside(row + k, start + branch))


def into(target, shift, to):
    def emit(row, value):
        target[row - shift, to, :] = value.astype(target.dtype)

    return emit


OTHER = slice(CH, 2 * CH)
HIDDEN = pltpu.VMEM((16, CH, LANES), jnp.bfloat16)
STACK = pltpu.VMEM((16, 2 * CH, LANES), jnp.bfloat16)


def merge_own(near_side, far_side, own, two, tables):
    def body(near_r, far_r, own_r, two_r, pair, mixed, cols, out, stack, hid):
        for slot, frame in enumerate((own_r, two_r)):
            fill(stack, slot, near_r, 0, slot)
            fill(stack, slot, frame, HALO)
            fill(stack, slot, far_r, HALO + ROWS, slot)
        level = Level(pair, mixed, cols, position() // 2, hid)
        level.first(stack, 0, 1, 15)
        level.second(stack, 0, 2, 14, into(out, 2, slice(None)))

    return pl.pallas_call(
        body,
        out_shape=array(12, CH, LANES),
        in_specs=[VMEM] * 7,
        out_specs=VMEM,
        scratch_shapes=[STACK, HIDDEN],
        compiler_params=SMALL,
        name="merge_own",
    )(near_side, far_side, own, two, *tables)


def merge_inner(near_side, one, three, mine, tables):
    def body(near_r, one_r, three_r, mine_r, pair, mixed, cols, hid_end, ones_end, top_end, done, stack, ones, hid, top_hid):
        for slot, frame in enumerate((one_r, three_r)):
            fill(stack, slot, near_r, 0, slot)
            fill(stack, slot, frame, HALO)
        fill(ones, 0, mine_r.at[0:8], 2)
        at = position()
        level = Level(pair, mixed, cols, at // 2, hid)
        level.first(stack, 0, 1, 11)
        level.second(stack, 0, 2, 10, into(ones, 0, OTHER))
        top = Level(pair, mixed, cols, at % 2, top_hid)
        top.first(ones, 0, 3, 9)
        top.second(ones, 0, 4, 8, into(done, 4, slice(None)))
        hid_end[...] = hid[9:11]
        ones_end[...] = ones[8:10]
        top_end[...] = top_hid[7:9]

    return pl.pallas_call(
        body,
        out_shape=(array(2, CH, LANES), array(2, 2 * CH, LANES), array(2, CH, LANES), array(4, CH, LANES, dtype=jnp.float32)),
        in_specs=[VMEM] * 7,
        out_specs=(VMEM,) * 4,
        scratch_shapes=[STACK, STACK, HIDDEN, HIDDEN],
        compiler_params=SMALL,
        name="merge_inner",
    )(near_side, one, three, mine, *tables)


def merge_outer(far_side, one, three, mine, inner, tables):
    def body(far_r, one_r, three_r, mine_r, hid_end, ones_end, top_end, done, pair, mixed, cols, out, stack, ones, hid, top_hid, rows, wide):
        for slot, frame in enumerate((one_r, three_r)):
            fill(stack, slot, frame.at[6:8], 10)
            fill(stack, slot, far_r, HALO + ROWS, slot)
        hid[9:11] = hid_end[...]
        ones[8:10] = ones_end[...]
        fill(ones, 0, mine_r.at[8:12], 10)
        top_hid[7:9] = top_end[...]
        rows[0:4] = done[...]
        at = position()
        level = Level(pair, mixed, cols, at // 2, hid)
        level.first(stack, 0, 11, 15)
        level.second(stack, 0, 10, 14, into(ones, 0, OTHER))
        top = Level(pair, mixed, cols, at % 2, top_hid)
        top.first(ones, 0, 9, 13)
        top.second(ones, 0, 8, 12, into(rows, 4, slice(None)))
        turn = 7 - 7 * odd_row()
        sign = 2 * odd_row() - 1
        for row in range(ROWS):
            wide[pl.ds(row, CH, stride=ROWS), :] = rows[turn + sign * row]
        out[...] = wide[...].reshape(CH, ROWS, LANES).astype(jnp.bfloat16)

    return pl.pallas_call(
        body,
        out_shape=array(CH, ROWS, LANES),
        in_specs=[VMEM] * 11,
        scratch_shapes=[
            STACK,
            STACK,
            HIDDEN,
            HIDDEN,
            pltpu.VMEM((ROWS, CH, LANES), jnp.float32),
            pltpu.VMEM((CH * ROWS, LANES), jnp.float32),
        ],
        compiler_params=SMALL,
        name="merge_outer",
    )(far_side, one, three, mine, *inner, *tables)


def on_device(frames, w_pair, w_mixed, slope_pair, slope_mixed):
    count = lax.axis_size("frame")
    quarter = count // 4
    rows = lax.axis_size("row")

    def swapped(block, mask):
        return lax.ppermute(block, "frame", [(i, i ^ (mask * quarter)) for i in range(count)])

    def on_chip(block):
        return lax.ppermute(block, "row", [(i, i ^ 1) for i in range(rows)])

    def off_chip(block):
        return lax.ppermute(block, "row", [(i, ((i + 1) ^ 1) - 1) for i in range(1, rows - 1)])

    own, one, three, two = spread(frames)
    one = swapped(one, 1)
    three = swapped(three, 3)
    two = swapped(two, 2)
    tables = weights(w_pair, w_mixed, slope_pair, slope_mixed)
    near_early, far_early = edges(own, two)
    far_early = off_chip(far_early)
    near_early = on_chip(near_early)
    near_late, far_late = edges(one, three)
    far_late = off_chip(far_late)
    near_late = on_chip(near_late)
    mine = merge_own(near_early, far_early, own, two, tables)
    inner = merge_inner(near_late, one, three, mine, tables)
    merged = merge_outer(far_late, one, three, mine, inner, tables)
    return merged[None]


def solution(mesh):
    placed = (P("frame", None, "row", None), P(), P(), P(), P())
    return jax.shard_map(
        on_device,
        mesh=mesh,
        in_specs=placed,
        out_specs=P("frame", None, "row", None),
        check_vma=False,
    )
```

```python
import jax
import jax.numpy as jnp
from jax import lax
from jax.experimental import pallas as pl
from jax.experimental.pallas import tpu as pltpu
from jax.sharding import PartitionSpec as P


ROWS = 8
HALO = 4
CH = 64
LANES = 128
PIECES = 4
VMEM = pl.BlockSpec(memory_space=pltpu.VMEM)
SMALL = pltpu.CompilerParams(vmem_limit_bytes=8 << 20)


def array(*shape, dtype=jnp.bfloat16):
    return jax.ShapeDtypeStruct(shape, dtype)


def position():
    return lax.axis_index("frame") // (lax.axis_size("frame") // 4)


def odd_row():
    return lax.axis_index("row") % 2


def spread(frames):
    def body(src, own, one, three, two, wide):
        at = position()
        turn = 7 - 7 * odd_row()
        sign = 2 * odd_row() - 1
        for k, out in ((2, two), (1, one), (3, three), (0, own)):
            wide[k] = src[at ^ k].astype(jnp.float32).reshape(CH * ROWS, LANES)
            for row in range(ROWS):
                out[turn + sign * row] = wide[k, pl.ds(row, CH, stride=ROWS), :].astype(jnp.bfloat16)

    return pl.pallas_call(
        body,
        out_shape=(array(ROWS, CH, LANES),) * 4,
        in_specs=[VMEM],
        out_specs=(VMEM,) * 4,
        scratch_shapes=[pltpu.VMEM((4, CH * ROWS, LANES), jnp.float32)],
        compiler_params=SMALL,
        name="spread",
    )(frames)


def weights(w_pair, w_mixed, slope_pair, slope_mixed):
    def body(wp, wm, sp, sm, pair, mixed, cols):
        top = 2 - 2 * odd_row()
        taps = (top, 1, 2 - top)
        for ky in range(3):
            at = ky * 2 * CH
            tap = wp[taps[ky]]
            pair[0, :, at : at + 2 * CH] = tap
            pair[1, :, at : at + 2 * CH] = jnp.concatenate([tap[:, CH:], tap[:, :CH]], axis=1)
        mixed[...] = jnp.concatenate([wm[taps[0]], wm[1], wm[taps[2]]], axis=1)
        square = lax.broadcasted_iota(jnp.int32, (CH, CH), 0) == lax.broadcasted_iota(jnp.int32, (CH, CH), 1)
        for k, slope in enumerate((sp, sm)):
            column = jnp.sum(jnp.where(square, slope[...], 0.0), axis=1, keepdims=True)
            cols[k] = jnp.broadcast_to(column, (CH, LANES))

    return pl.pallas_call(
        body,
        out_shape=(array(2, 3 * CH, 6 * CH), array(3 * CH, 3 * CH), array(2, CH, LANES, dtype=jnp.float32)),
        in_specs=[VMEM] * 4,
        out_specs=(VMEM,) * 3,
        compiler_params=SMALL,
        name="weights",
    )(w_pair.reshape(3, 3 * CH, 2 * CH), w_mixed.reshape(3, 3 * CH, CH), slope_pair.reshape(1, CH), slope_mixed.reshape(1, CH))


def edges(*frames):
    def body(*refs):
        near_side, far_side = refs[-2:]
        for k, frame in enumerate(refs[:-2]):
            for row in range(HALO):
                near_side[row, k * CH : (k + 1) * CH, :] = frame[HALO - 1 - row]
                far_side[row, k * CH : (k + 1) * CH, :] = frame[ROWS - 1 - row]

    half = array(HALO, len(frames) * CH, LANES)
    return pl.pallas_call(
        body,
        out_shape=(half, half),
        in_specs=[VMEM] * len(frames),
        out_specs=(VMEM,) * 2,
        compiler_params=SMALL,
        name="edges",
    )(*frames)


def fill(stack, slot, source, at, part=0):
    to = slice(slot * CH, (slot + 1) * CH)
    stack[at : at + source.shape[0], to, :] = source[:, part * CH : (part + 1) * CH, :]


class Level:
    def __init__(self, pair, mixed, cols, swap, hid):
        lane = lax.broadcasted_iota(jnp.int32, (CH, LANES), 1)
        self.not_first = lane > 0
        self.not_last = lane < LANES - 1
        self.pair = pair[swap]
        self.mixed = mixed[...]
        self.cols = cols
        self.swap = swap
        self.hid = hid
        place = lax.axis_index("row")
        self.edge = (place == 0) | (place == lax.axis_size("row") - 1)

    def inside(self, row, value):
        return jnp.where(self.edge, 0.0, value) if row >= HALO + ROWS else value

    def fold(self, part, which):
        left = jnp.where(self.not_first, pltpu.roll(part[:CH], 1, 1), 0.0)
        right = jnp.where(self.not_last, pltpu.roll(part[2 * CH :], LANES - 1, 1), 0.0)
        total = part[CH : 2 * CH] + left + right
        return jnp.maximum(total, self.cols[which] * total)

    def product(self, lhs, stack, row, depth):
        rhs = jnp.concatenate([stack[r - 1 : r + 2].reshape(3 * depth, LANES) for r in (row, row + 1)], axis=1)
        return jnp.dot(lhs, rhs, preferred_element_type=jnp.float32)

    def first(self, stack, shift, low, high):
        for row in range(low, high, 2):
            both = self.product(self.pair, stack, row - shift, 2 * CH)
            for k in range(2):
                value = self.fold(both[:, k * LANES : (k + 1) * LANES], 0)
                self.hid[row + k] = self.inside(row + k, value).astype(jnp.bfloat16)

    def second(self, stack, shift, low, high, emit):
        for row in range(low, high, 2):
            both = self.product(self.mixed, self.hid, row, CH)
            for k in range(2):
                start = stack[row + k - shift, pl.ds(self.swap * CH, CH), :].astype(jnp.float32)
                branch = self.fold(both[:, k * LANES : (k + 1) * LANES], 1)
                emit(row + k, self.inside(row + k, start + branch))


def into(target, shift, to):
    def emit(row, value):
        target[row - shift, to, :] = value.astype(target.dtype)

    return emit


OTHER = slice(CH, 2 * CH)
HIDDEN = pltpu.VMEM((16, CH, LANES), jnp.bfloat16)
STACK = pltpu.VMEM((16, 2 * CH, LANES), jnp.bfloat16)


def merge_own(near_side, far_side, own, two, tables):
    def body(near_r, far_r, own_r, two_r, pair, mixed, cols, out, stack, hid):
        for slot, frame in enumerate((own_r, two_r)):
            fill(stack, slot, near_r, 0, slot)
            fill(stack, slot, frame, HALO)
            fill(stack, slot, far_r, HALO + ROWS, slot)
        level = Level(pair, mixed, cols, position() // 2, hid)
        level.first(stack, 0, 1, 15)
        level.second(stack, 0, 2, 14, into(out, 2, slice(None)))

    return pl.pallas_call(
        body,
        out_shape=array(12, CH, LANES),
        in_specs=[VMEM] * 7,
        out_specs=VMEM,
        scratch_shapes=[STACK, HIDDEN],
        compiler_params=SMALL,
        name="merge_own",
    )(near_side, far_side, own, two, *tables)


def merge_inner(near_side, one, three, mine, tables):
    def body(near_r, one_r, three_r, mine_r, pair, mixed, cols, hid_end, ones_end, top_end, done, stack, ones, hid, top_hid):
        for slot, frame in enumerate((one_r, three_r)):
            fill(stack, slot, near_r, 0, slot)
            fill(stack, slot, frame, HALO)
        fill(ones, 0, mine_r.at[0:8], 2)
        at = position()
        level = Level(pair, mixed, cols, at // 2, hid)
        level.first(stack, 0, 1, 11)
        level.second(stack, 0, 2, 10, into(ones, 0, OTHER))
        top = Level(pair, mixed, cols, at % 2, top_hid)
        top.first(ones, 0, 3, 9)
        top.second(ones, 0, 4, 8, into(done, 4, slice(None)))
        hid_end[...] = hid[9:11]
        ones_end[...] = ones[8:10]
        top_end[...] = top_hid[7:9]

    return pl.pallas_call(
        body,
        out_shape=(array(2, CH, LANES), array(2, 2 * CH, LANES), array(2, CH, LANES), array(4, CH, LANES, dtype=jnp.float32)),
        in_specs=[VMEM] * 7,
        out_specs=(VMEM,) * 4,
        scratch_shapes=[STACK, STACK, HIDDEN, HIDDEN],
        compiler_params=SMALL,
        name="merge_inner",
    )(near_side, one, three, mine, *tables)


def merge_outer(far_side, one, three, mine, inner, tables):
    def body(far_r, one_r, three_r, mine_r, hid_end, ones_end, top_end, done, pair, mixed, cols, out, stack, ones, hid, top_hid, rows, wide, held, sems):
        for slot, frame in enumerate((one_r, three_r)):
            fill(stack, slot, frame.at[6:8], 10)
            fill(stack, slot, far_r, HALO + ROWS, slot)
        hid[9:11] = hid_end[...]
        ones[8:10] = ones_end[...]
        fill(ones, 0, mine_r.at[8:12], 10)
        top_hid[7:9] = top_end[...]
        rows[0:4] = done[...]
        at = position()
        level = Level(pair, mixed, cols, at // 2, hid)
        level.first(stack, 0, 11, 15)
        level.second(stack, 0, 10, 14, into(ones, 0, OTHER))
        top = Level(pair, mixed, cols, at % 2, top_hid)
        top.first(ones, 0, 9, 13)
        top.second(ones, 0, 8, 12, into(rows, 4, slice(None)))
        turn = 7 - 7 * odd_row()
        sign = 2 * odd_row() - 1
        for row in range(ROWS):
            wide[pl.ds(row, CH, stride=ROWS), :] = rows[turn + sign * row]
        copies = []
        for k in range(PIECES):
            some = slice(k * CH // PIECES, (k + 1) * CH // PIECES)
            part = wide[some.start * ROWS : some.stop * ROWS, :]
            held[some] = part.reshape(CH // PIECES, ROWS, LANES).astype(jnp.bfloat16)
            copies.append(pltpu.make_async_copy(held.at[some], out.at[some], sems.at[k]))
            copies[k].start()
        for copy in copies:
            copy.wait()

    return pl.pallas_call(
        body,
        out_shape=array(CH, ROWS, LANES),
        in_specs=[VMEM] * 11,
        out_specs=pl.BlockSpec(memory_space=pl.ANY),
        scratch_shapes=[
            STACK,
            STACK,
            HIDDEN,
            HIDDEN,
            pltpu.VMEM((ROWS, CH, LANES), jnp.float32),
            pltpu.VMEM((CH * ROWS, LANES), jnp.float32),
            pltpu.VMEM((CH, ROWS, LANES), jnp.bfloat16),
            pltpu.SemaphoreType.DMA((PIECES,)),
        ],
        compiler_params=SMALL,
        name="merge_outer",
    )(far_side, one, three, mine, *inner, *tables)


def on_device(frames, w_pair, w_mixed, slope_pair, slope_mixed):
    count = lax.axis_size("frame")
    quarter = count // 4
    rows = lax.axis_size("row")

    def swapped(block, mask):
        return lax.ppermute(block, "frame", [(i, i ^ (mask * quarter)) for i in range(count)])

    def on_chip(block):
        return lax.ppermute(block, "row", [(i, i ^ 1) for i in range(rows)])

    def off_chip(block):
        return lax.ppermute(block, "row", [(i, ((i + 1) ^ 1) - 1) for i in range(1, rows - 1)])

    own, one, three, two = spread(frames)
    one = swapped(one, 1)
    three = swapped(three, 3)
    two = swapped(two, 2)
    tables = weights(w_pair, w_mixed, slope_pair, slope_mixed)
    near_early, far_early = edges(own, two)
    far_early = off_chip(far_early)
    near_early = on_chip(near_early)
    near_late, far_late = edges(one, three)
    far_late = off_chip(far_late)
    near_late = on_chip(near_late)
    mine = merge_own(near_early, far_early, own, two, tables)
    inner = merge_inner(near_late, one, three, mine, tables)
    merged = merge_outer(far_late, one, three, mine, inner, tables)
    return merged[None]


def solution(mesh):
    placed = (P("frame", None, "row", None), P(), P(), P(), P())
    return jax.shard_map(
        on_device,
        mesh=mesh,
        in_specs=placed,
        out_specs=P("frame", None, "row", None),
        check_vma=False,
    )
```

```python
from functools import partial

import jax
import jax.numpy as jnp
from jax import lax
from jax.experimental import pallas as pl
from jax.experimental.pallas import tpu as pltpu
from jax.sharding import PartitionSpec as P


ROWS = 8
HALO = 4
CH = 64
LANES = 128
FRONT = 54800
VMEM = pl.BlockSpec(memory_space=pltpu.VMEM)
SMALL = pltpu.CompilerParams(vmem_limit_bytes=8 << 20)


def array(*shape, dtype=jnp.bfloat16):
    return jax.ShapeDtypeStruct(shape, dtype)


def position():
    return lax.axis_index("frame") // (lax.axis_size("frame") // 4)


def odd_row():
    return lax.axis_index("row") % 2


def lead(frames):
    def body(src, two, held, wide, sem):
        copy = pltpu.make_async_copy(src.at[position() ^ 2], held, sem)
        copy.start()
        copy.wait()
        rows_first(held[...], wide, two)

    return pl.pallas_call(
        body,
        out_shape=array(ROWS, CH, LANES),
        in_specs=[pl.BlockSpec(memory_space=pl.ANY)],
        out_specs=VMEM,
        scratch_shapes=[
            pltpu.VMEM((CH, ROWS, LANES), jnp.bfloat16),
            pltpu.VMEM((CH * ROWS, LANES), jnp.float32),
            pltpu.SemaphoreType.DMA,
        ],
        compiler_params=pltpu.CompilerParams(vmem_limit_bytes=FRONT << 10),
        name="lead",
    )(frames)


def rows_first(frame, wide, out):
    wide[...] = frame.astype(jnp.float32).reshape(CH * ROWS, LANES)
    turn = 7 - 7 * odd_row()
    sign = 2 * odd_row() - 1
    for row in range(ROWS):
        out[turn + sign * row] = wide[pl.ds(row, CH, stride=ROWS), :].astype(jnp.bfloat16)


def spread(frames):
    def body(src, own, one, three, wide):
        at = position()
        for k, out in ((1, one), (3, three), (0, own)):
            rows_first(src[at ^ k], wide.at[k], out)

    return pl.pallas_call(
        body,
        out_shape=(array(ROWS, CH, LANES),) * 3,
        in_specs=[VMEM],
        out_specs=(VMEM,) * 3,
        scratch_shapes=[pltpu.VMEM((4, CH * ROWS, LANES), jnp.float32)],
        compiler_params=SMALL,
        name="spread",
    )(frames)


def weights(w_pair, w_mixed, slope_pair, slope_mixed):
    def body(wp, wm, sp, sm, pair, mixed, cols):
        top = 2 - 2 * odd_row()
        taps = (top, 1, 2 - top)
        for ky in range(3):
            at = ky * 2 * CH
            tap = wp[taps[ky]]
            pair[0, :, at : at + 2 * CH] = tap
            pair[1, :, at : at + 2 * CH] = jnp.concatenate([tap[:, CH:], tap[:, :CH]], axis=1)
        mixed[...] = jnp.concatenate([wm[taps[0]], wm[1], wm[taps[2]]], axis=1)
        square = lax.broadcasted_iota(jnp.int32, (CH, CH), 0) == lax.broadcasted_iota(jnp.int32, (CH, CH), 1)
        for k, slope in enumerate((sp, sm)):
            column = jnp.sum(jnp.where(square, slope[...], 0.0), axis=1, keepdims=True)
            cols[k] = jnp.broadcast_to(column, (CH, LANES))

    return pl.pallas_call(
        body,
        out_shape=(array(2, 3 * CH, 6 * CH), array(3 * CH, 3 * CH), array(2, CH, LANES, dtype=jnp.float32)),
        in_specs=[VMEM] * 4,
        out_specs=(VMEM,) * 3,
        compiler_params=SMALL,
        name="weights",
    )(w_pair.reshape(3, 3 * CH, 2 * CH), w_mixed.reshape(3, 3 * CH, CH), slope_pair.reshape(1, CH), slope_mixed.reshape(1, CH))


def edges(*frames):
    def body(*refs):
        near_side, far_side = refs[-2:]
        for k, frame in enumerate(refs[:-2]):
            for row in range(HALO):
                near_side[row, k * CH : (k + 1) * CH, :] = frame[HALO - 1 - row]
                far_side[row, k * CH : (k + 1) * CH, :] = frame[ROWS - 1 - row]

    half = array(HALO, len(frames) * CH, LANES)
    return pl.pallas_call(
        body,
        out_shape=(half, half),
        in_specs=[VMEM] * len(frames),
        out_specs=(VMEM,) * 2,
        compiler_params=SMALL,
        name="edges",
    )(*frames)


def fill(stack, slot, source, at, part=0):
    to = slice(slot * CH, (slot + 1) * CH)
    stack[at : at + source.shape[0], to, :] = source[:, part * CH : (part + 1) * CH, :]


def at_seam():
    row = lax.axis_index("row")
    half = lax.axis_size("row") // 2
    return (row == half) | (row == half - 1)


class Level:
    def __init__(self, pair, mixed, cols, swap, hid):
        lane = lax.broadcasted_iota(jnp.int32, (CH, LANES), 1)
        self.not_first = lane > 0
        self.not_last = lane < LANES - 1
        self.pair = pair[swap]
        self.mixed = mixed[...]
        self.cols = cols
        self.swap = swap
        self.hid = hid
        place = lax.axis_index("row")
        self.edge = (place == 0) | (place == lax.axis_size("row") - 1)

    def inside(self, row, value):
        return jnp.where(self.edge, 0.0, value) if row >= HALO + ROWS else value

    def fold(self, part, which):
        left = jnp.where(self.not_first, pltpu.roll(part[:CH], 1, 1), 0.0)
        right = jnp.where(self.not_last, pltpu.roll(part[2 * CH :], LANES - 1, 1), 0.0)
        total = part[CH : 2 * CH] + left + right
        return jnp.maximum(total, self.cols[which] * total)

    def product(self, lhs, stack, row, depth):
        rhs = jnp.concatenate([stack[r - 1 : r + 2].reshape(3 * depth, LANES) for r in (row, row + 1)], axis=1)
        return jnp.dot(lhs, rhs, preferred_element_type=jnp.float32)

    def first(self, stack, shift, low, high):
        for row in range(low, high, 2):
            both = self.product(self.pair, stack, row - shift, 2 * CH)
            for k in range(2):
                value = self.fold(both[:, k * LANES : (k + 1) * LANES], 0)
                self.hid[row + k] = self.inside(row + k, value).astype(jnp.bfloat16)

    def second(self, stack, shift, low, high, emit):
        for row in range(low, high, 2):
            both = self.product(self.mixed, self.hid, row, CH)
            for k in range(2):
                start = stack[row + k - shift, pl.ds(self.swap * CH, CH), :].astype(jnp.float32)
                branch = self.fold(both[:, k * LANES : (k + 1) * LANES], 1)
                emit(row + k, self.inside(row + k, start + branch))


def into(target, shift, to):
    def emit(row, value):
        target[row - shift, to, :] = value.astype(target.dtype)

    return emit


OTHER = slice(CH, 2 * CH)
HIDDEN = pltpu.VMEM((16, CH, LANES), jnp.bfloat16)
STACK = pltpu.VMEM((16, 2 * CH, LANES), jnp.bfloat16)


def merge_own(near_side, far_side, own, two, tables):
    def body(near_r, far_r, own_r, two_r, pair, mixed, cols, out, stack, hid):
        for slot, frame in enumerate((own_r, two_r)):
            fill(stack, slot, near_r, 0, slot)
            fill(stack, slot, frame, HALO)
            fill(stack, slot, far_r, HALO + ROWS, slot)
        level = Level(pair, mixed, cols, position() // 2, hid)
        level.first(stack, 0, 1, 15)
        level.second(stack, 0, 2, 14, into(out, 2, slice(None)))

    return pl.pallas_call(
        body,
        out_shape=array(12, CH, LANES),
        in_specs=[VMEM] * 7,
        out_specs=VMEM,
        scratch_shapes=[STACK, HIDDEN],
        compiler_params=SMALL,
        name="merge_own",
    )(near_side, far_side, own, two, *tables)


def merge_inner(near_side, one, three, mine, tables):
    def body(*refs):
        pl.when(at_seam())(partial(inner, *refs))

    def inner(near_r, one_r, three_r, mine_r, pair, mixed, cols, hid_end, ones_end, top_end, done, stack, ones, hid, top_hid):
        for slot, frame in enumerate((one_r, three_r)):
            fill(stack, slot, near_r, 0, slot)
            fill(stack, slot, frame, HALO)
        fill(ones, 0, mine_r.at[0:8], 2)
        at = position()
        level = Level(pair, mixed, cols, at // 2, hid)
        level.first(stack, 0, 1, 11)
        level.second(stack, 0, 2, 10, into(ones, 0, OTHER))
        top = Level(pair, mixed, cols, at % 2, top_hid)
        top.first(ones, 0, 3, 9)
        top.second(ones, 0, 4, 8, into(done, 4, slice(None)))
        hid_end[...] = hid[9:11]
        ones_end[...] = ones[8:10]
        top_end[...] = top_hid[7:9]

    return pl.pallas_call(
        body,
        out_shape=(array(2, CH, LANES), array(2, 2 * CH, LANES), array(2, CH, LANES), array(4, CH, LANES, dtype=jnp.float32)),
        in_specs=[VMEM] * 7,
        out_specs=(VMEM,) * 4,
        scratch_shapes=[STACK, STACK, HIDDEN, HIDDEN],
        compiler_params=SMALL,
        name="merge_inner",
    )(near_side, one, three, mine, *tables)


def merge_outer(near_side, far_side, one, three, mine, inner, tables):
    def body(near_r, far_r, one_r, three_r, mine_r, hid_end, ones_end, top_end, done, pair, mixed, cols, out, stack, ones, hid, top_hid, rows, wide):
        at = position()

        @pl.when(at_seam())
        def _():
            for slot, frame in enumerate((one_r, three_r)):
                fill(stack, slot, frame.at[6:8], 10)
                fill(stack, slot, far_r, HALO + ROWS, slot)
            hid[9:11] = hid_end[...]
            ones[8:10] = ones_end[...]
            fill(ones, 0, mine_r.at[8:12], 10)
            top_hid[7:9] = top_end[...]
            rows[0:4] = done[...]
            level = Level(pair, mixed, cols, at // 2, hid)
            level.first(stack, 0, 11, 15)
            level.second(stack, 0, 10, 14, into(ones, 0, OTHER))
            top = Level(pair, mixed, cols, at % 2, top_hid)
            top.first(ones, 0, 9, 13)
            top.second(ones, 0, 8, 12, into(rows, 4, slice(None)))

        @pl.when(jnp.logical_not(at_seam()))
        def _():
            for slot, frame in enumerate((one_r, three_r)):
                fill(stack, slot, near_r, 0, slot)
                fill(stack, slot, frame, HALO)
                fill(stack, slot, far_r, HALO + ROWS, slot)
            fill(ones, 0, mine_r, 2)
            level = Level(pair, mixed, cols, at // 2, hid)
            level.first(stack, 0, 1, 15)
            level.second(stack, 0, 2, 14, into(ones, 0, OTHER))
            top = Level(pair, mixed, cols, at % 2, top_hid)
            top.first(ones, 0, 3, 13)
            top.second(ones, 0, 4, 12, into(rows, 4, slice(None)))

        turn = 7 - 7 * odd_row()
        sign = 2 * odd_row() - 1
        for row in range(ROWS):
            wide[pl.ds(row, CH, stride=ROWS), :] = rows[turn + sign * row]
        out[...] = wide[...].reshape(CH, ROWS, LANES).astype(jnp.bfloat16)

    return pl.pallas_call(
        body,
        out_shape=array(CH, ROWS, LANES),
        in_specs=[VMEM] * 12,
        scratch_shapes=[
            STACK,
            STACK,
            HIDDEN,
            HIDDEN,
            pltpu.VMEM((ROWS, CH, LANES), jnp.float32),
            pltpu.VMEM((CH * ROWS, LANES), jnp.float32),
        ],
        compiler_params=SMALL,
        name="merge_outer",
    )(near_side, far_side, one, three, mine, *inner, *tables)


def on_device(frames, w_pair, w_mixed, slope_pair, slope_mixed):
    count = lax.axis_size("frame")
    quarter = count // 4
    rows = lax.axis_size("row")

    def swapped(block, mask):
        return lax.ppermute(block, "frame", [(i, i ^ (mask * quarter)) for i in range(count)])

    def on_chip(block):
        return lax.ppermute(block, "row", [(i, i ^ 1) for i in range(rows)])

    def off_chip(block):
        return lax.ppermute(block, "row", [(i, ((i + 1) ^ 1) - 1) for i in range(1, rows - 1)])

    two = lead(frames)
    own, one, three = spread(frames)
    one = swapped(one, 1)
    three = swapped(three, 3)
    two = swapped(two, 2)
    tables = weights(w_pair, w_mixed, slope_pair, slope_mixed)
    near_early, far_early = edges(own, two)
    far_early = off_chip(far_early)
    near_early = on_chip(near_early)
    near_late, far_late = edges(one, three)
    far_late = off_chip(far_late)
    near_late = on_chip(near_late)
    mine = merge_own(near_early, far_early, own, two, tables)
    inner = merge_inner(near_late, one, three, mine, tables)
    merged = merge_outer(near_late, far_late, one, three, mine, inner, tables)
    return merged[None]


def solution(mesh):
    placed = (P("frame", None, "row", None), P(), P(), P(), P())
    return jax.shard_map(
        on_device,
        mesh=mesh,
        in_specs=placed,
        out_specs=P("frame", None, "row", None),
        check_vma=False,
    )
```

```python
from functools import partial

import jax
import jax.numpy as jnp
from jax import lax
from jax.experimental import pallas as pl
from jax.experimental.pallas import tpu as pltpu
from jax.sharding import PartitionSpec as P


ROWS = 8
HALO = 4
CH = 64
LANES = 128
PIECES = 8
FRONT = 54800
VMEM = pl.BlockSpec(memory_space=pltpu.VMEM)
SMALL = pltpu.CompilerParams(vmem_limit_bytes=8 << 20)


def array(*shape, dtype=jnp.bfloat16):
    return jax.ShapeDtypeStruct(shape, dtype)


def position():
    return lax.axis_index("frame") // (lax.axis_size("frame") // 4)


def odd_row():
    return lax.axis_index("row") % 2


def lead(frames):
    def body(src, two, held, wide, sems):
        copies = []
        for k in range(PIECES):
            some = pl.ds(k * CH // PIECES, CH // PIECES)
            copies.append(pltpu.make_async_copy(src.at[position() ^ 2, some], held.at[some], sems.at[k]))
            copies[k].start()
        for copy in copies:
            copy.wait()
        rows_first(held[...], wide, two)

    return pl.pallas_call(
        body,
        out_shape=array(ROWS, CH, LANES),
        in_specs=[pl.BlockSpec(memory_space=pl.ANY)],
        out_specs=VMEM,
        scratch_shapes=[
            pltpu.VMEM((CH, ROWS, LANES), jnp.bfloat16),
            pltpu.VMEM((CH * ROWS, LANES), jnp.float32),
            pltpu.SemaphoreType.DMA((PIECES,)),
        ],
        compiler_params=pltpu.CompilerParams(vmem_limit_bytes=FRONT << 10),
        name="lead",
    )(frames)


def rows_first(frame, wide, out):
    wide[...] = frame.astype(jnp.float32).reshape(CH * ROWS, LANES)
    turn = 7 - 7 * odd_row()
    sign = 2 * odd_row() - 1
    for row in range(ROWS):
        out[turn + sign * row] = wide[pl.ds(row, CH, stride=ROWS), :].astype(jnp.bfloat16)


def spread(frames):
    def body(src, own, one, three, wide):
        at = position()
        for k, out in ((1, one), (3, three), (0, own)):
            rows_first(src[at ^ k], wide.at[k], out)

    return pl.pallas_call(
        body,
        out_shape=(array(ROWS, CH, LANES),) * 3,
        in_specs=[VMEM],
        out_specs=(VMEM,) * 3,
        scratch_shapes=[pltpu.VMEM((4, CH * ROWS, LANES), jnp.float32)],
        compiler_params=SMALL,
        name="spread",
    )(frames)


def weights(w_pair, w_mixed, slope_pair, slope_mixed):
    def body(wp, wm, sp, sm, pair, mixed, cols):
        top = 2 - 2 * odd_row()
        taps = (top, 1, 2 - top)
        for ky in range(3):
            at = ky * 2 * CH
            tap = wp[taps[ky]]
            pair[0, :, at : at + 2 * CH] = tap
            pair[1, :, at : at + 2 * CH] = jnp.concatenate([tap[:, CH:], tap[:, :CH]], axis=1)
        mixed[...] = jnp.concatenate([wm[taps[0]], wm[1], wm[taps[2]]], axis=1)
        square = lax.broadcasted_iota(jnp.int32, (CH, CH), 0) == lax.broadcasted_iota(jnp.int32, (CH, CH), 1)
        for k, slope in enumerate((sp, sm)):
            column = jnp.sum(jnp.where(square, slope[...], 0.0), axis=1, keepdims=True)
            cols[k] = jnp.broadcast_to(column, (CH, LANES))

    return pl.pallas_call(
        body,
        out_shape=(array(2, 3 * CH, 6 * CH), array(3 * CH, 3 * CH), array(2, CH, LANES, dtype=jnp.float32)),
        in_specs=[VMEM] * 4,
        out_specs=(VMEM,) * 3,
        compiler_params=SMALL,
        name="weights",
    )(w_pair.reshape(3, 3 * CH, 2 * CH), w_mixed.reshape(3, 3 * CH, CH), slope_pair.reshape(1, CH), slope_mixed.reshape(1, CH))


def edges(*frames):
    def body(*refs):
        near_side, far_side = refs[-2:]
        for k, frame in enumerate(refs[:-2]):
            for row in range(HALO):
                near_side[row, k * CH : (k + 1) * CH, :] = frame[HALO - 1 - row]
                far_side[row, k * CH : (k + 1) * CH, :] = frame[ROWS - 1 - row]

    half = array(HALO, len(frames) * CH, LANES)
    return pl.pallas_call(
        body,
        out_shape=(half, half),
        in_specs=[VMEM] * len(frames),
        out_specs=(VMEM,) * 2,
        compiler_params=SMALL,
        name="edges",
    )(*frames)


def fill(stack, slot, source, at, part=0):
    to = slice(slot * CH, (slot + 1) * CH)
    stack[at : at + source.shape[0], to, :] = source[:, part * CH : (part + 1) * CH, :]


def at_seam():
    row = lax.axis_index("row")
    half = lax.axis_size("row") // 2
    return (row == half) | (row == half - 1)


class Level:
    def __init__(self, pair, mixed, cols, swap, hid):
        lane = lax.broadcasted_iota(jnp.int32, (CH, LANES), 1)
        self.not_first = lane > 0
        self.not_last = lane < LANES - 1
        self.pair = pair[swap]
        self.mixed = mixed[...]
        self.cols = cols
        self.swap = swap
        self.hid = hid
        place = lax.axis_index("row")
        self.edge = (place == 0) | (place == lax.axis_size("row") - 1)

    def inside(self, row, value):
        return jnp.where(self.edge, 0.0, value) if row >= HALO + ROWS else value

    def fold(self, part, which):
        left = jnp.where(self.not_first, pltpu.roll(part[:CH], 1, 1), 0.0)
        right = jnp.where(self.not_last, pltpu.roll(part[2 * CH :], LANES - 1, 1), 0.0)
        total = part[CH : 2 * CH] + left + right
        return jnp.maximum(total, self.cols[which] * total)

    def product(self, lhs, stack, row, depth):
        rhs = jnp.concatenate([stack[r - 1 : r + 2].reshape(3 * depth, LANES) for r in (row, row + 1)], axis=1)
        return jnp.dot(lhs, rhs, preferred_element_type=jnp.float32)

    def first(self, stack, shift, low, high):
        for row in range(low, high, 2):
            both = self.product(self.pair, stack, row - shift, 2 * CH)
            for k in range(2):
                value = self.fold(both[:, k * LANES : (k + 1) * LANES], 0)
                self.hid[row + k] = self.inside(row + k, value).astype(jnp.bfloat16)

    def second(self, stack, shift, low, high, emit):
        for row in range(low, high, 2):
            both = self.product(self.mixed, self.hid, row, CH)
            for k in range(2):
                start = stack[row + k - shift, pl.ds(self.swap * CH, CH), :].astype(jnp.float32)
                branch = self.fold(both[:, k * LANES : (k + 1) * LANES], 1)
                emit(row + k, self.inside(row + k, start + branch))


def into(target, shift, to):
    def emit(row, value):
        target[row - shift, to, :] = value.astype(target.dtype)

    return emit


OTHER = slice(CH, 2 * CH)
HIDDEN = pltpu.VMEM((16, CH, LANES), jnp.bfloat16)
STACK = pltpu.VMEM((16, 2 * CH, LANES), jnp.bfloat16)


def merge_own(near_side, far_side, own, two, tables):
    def body(near_r, far_r, own_r, two_r, pair, mixed, cols, out, stack, hid):
        for slot, frame in enumerate((own_r, two_r)):
            fill(stack, slot, near_r, 0, slot)
            fill(stack, slot, frame, HALO)
            fill(stack, slot, far_r, HALO + ROWS, slot)
        level = Level(pair, mixed, cols, position() // 2, hid)
        level.first(stack, 0, 1, 15)
        level.second(stack, 0, 2, 14, into(out, 2, slice(None)))

    return pl.pallas_call(
        body,
        out_shape=array(12, CH, LANES),
        in_specs=[VMEM] * 7,
        out_specs=VMEM,
        scratch_shapes=[STACK, HIDDEN],
        compiler_params=SMALL,
        name="merge_own",
    )(near_side, far_side, own, two, *tables)


def merge_inner(near_side, one, three, mine, tables):
    def body(*refs):
        pl.when(at_seam())(partial(inner, *refs))

    def inner(near_r, one_r, three_r, mine_r, pair, mixed, cols, hid_end, ones_end, top_end, done, stack, ones, hid, top_hid):
        for slot, frame in enumerate((one_r, three_r)):
            fill(stack, slot, near_r, 0, slot)
            fill(stack, slot, frame, HALO)
        fill(ones, 0, mine_r.at[0:8], 2)
        at = position()
        level = Level(pair, mixed, cols, at // 2, hid)
        level.first(stack, 0, 1, 11)
        level.second(stack, 0, 2, 10, into(ones, 0, OTHER))
        top = Level(pair, mixed, cols, at % 2, top_hid)
        top.first(ones, 0, 3, 9)
        top.second(ones, 0, 4, 8, into(done, 4, slice(None)))
        hid_end[...] = hid[9:11]
        ones_end[...] = ones[8:10]
        top_end[...] = top_hid[7:9]

    return pl.pallas_call(
        body,
        out_shape=(array(2, CH, LANES), array(2, 2 * CH, LANES), array(2, CH, LANES), array(4, CH, LANES, dtype=jnp.float32)),
        in_specs=[VMEM] * 7,
        out_specs=(VMEM,) * 4,
        scratch_shapes=[STACK, STACK, HIDDEN, HIDDEN],
        compiler_params=SMALL,
        name="merge_inner",
    )(near_side, one, three, mine, *tables)


def merge_outer(near_side, far_side, one, three, mine, inner, tables):
    def body(near_r, far_r, one_r, three_r, mine_r, hid_end, ones_end, top_end, done, pair, mixed, cols, out, stack, ones, hid, top_hid, rows, wide):
        at = position()

        @pl.when(at_seam())
        def _():
            for slot, frame in enumerate((one_r, three_r)):
                fill(stack, slot, frame.at[6:8], 10)
                fill(stack, slot, far_r, HALO + ROWS, slot)
            hid[9:11] = hid_end[...]
            ones[8:10] = ones_end[...]
            fill(ones, 0, mine_r.at[8:12], 10)
            top_hid[7:9] = top_end[...]
            rows[0:4] = done[...]
            level = Level(pair, mixed, cols, at // 2, hid)
            level.first(stack, 0, 11, 15)
            level.second(stack, 0, 10, 14, into(ones, 0, OTHER))
            top = Level(pair, mixed, cols, at % 2, top_hid)
            top.first(ones, 0, 9, 13)
            top.second(ones, 0, 8, 12, into(rows, 4, slice(None)))

        @pl.when(jnp.logical_not(at_seam()))
        def _():
            for slot, frame in enumerate((one_r, three_r)):
                fill(stack, slot, near_r, 0, slot)
                fill(stack, slot, frame, HALO)
                fill(stack, slot, far_r, HALO + ROWS, slot)
            fill(ones, 0, mine_r, 2)
            level = Level(pair, mixed, cols, at // 2, hid)
            level.first(stack, 0, 1, 15)
            level.second(stack, 0, 2, 14, into(ones, 0, OTHER))
            top = Level(pair, mixed, cols, at % 2, top_hid)
            top.first(ones, 0, 3, 13)
            top.second(ones, 0, 4, 12, into(rows, 4, slice(None)))

        turn = 7 - 7 * odd_row()
        sign = 2 * odd_row() - 1
        for row in range(ROWS):
            wide[pl.ds(row, CH, stride=ROWS), :] = rows[turn + sign * row]
        out[...] = wide[...].reshape(CH, ROWS, LANES).astype(jnp.bfloat16)

    return pl.pallas_call(
        body,
        out_shape=array(CH, ROWS, LANES),
        in_specs=[VMEM] * 12,
        scratch_shapes=[
            STACK,
            STACK,
            HIDDEN,
            HIDDEN,
            pltpu.VMEM((ROWS, CH, LANES), jnp.float32),
            pltpu.VMEM((CH * ROWS, LANES), jnp.float32),
        ],
        compiler_params=SMALL,
        name="merge_outer",
    )(near_side, far_side, one, three, mine, *inner, *tables)


def on_device(frames, w_pair, w_mixed, slope_pair, slope_mixed):
    count = lax.axis_size("frame")
    quarter = count // 4
    rows = lax.axis_size("row")

    def swapped(block, mask):
        return lax.ppermute(block, "frame", [(i, i ^ (mask * quarter)) for i in range(count)])

    def on_chip(block):
        return lax.ppermute(block, "row", [(i, i ^ 1) for i in range(rows)])

    def off_chip(block):
        return lax.ppermute(block, "row", [(i, ((i + 1) ^ 1) - 1) for i in range(1, rows - 1)])

    two = lead(frames)
    own, one, three = spread(frames)
    one = swapped(one, 1)
    three = swapped(three, 3)
    two = swapped(two, 2)
    tables = weights(w_pair, w_mixed, slope_pair, slope_mixed)
    near_early, far_early = edges(own, two)
    far_early = off_chip(far_early)
    near_early = on_chip(near_early)
    near_late, far_late = edges(one, three)
    far_late = off_chip(far_late)
    near_late = on_chip(near_late)
    mine = merge_own(near_early, far_early, own, two, tables)
    inner = merge_inner(near_late, one, three, mine, tables)
    merged = merge_outer(near_late, far_late, one, three, mine, inner, tables)
    return merged[None]


def solution(mesh):
    placed = (P("frame", None, "row", None), P(), P(), P(), P())
    return jax.shard_map(
        on_device,
        mesh=mesh,
        in_specs=placed,
        out_specs=P("frame", None, "row", None),
        check_vma=False,
    )
```

```python
from functools import partial

import jax
import jax.numpy as jnp
from jax import lax
from jax.experimental import pallas as pl
from jax.experimental.pallas import tpu as pltpu
from jax.sharding import PartitionSpec as P


ROWS = 8
HALO = 4
CH = 64
LANES = 128
PIECES = 8
FRONT = 54800
VMEM = pl.BlockSpec(memory_space=pltpu.VMEM)
SMALL = pltpu.CompilerParams(vmem_limit_bytes=8 << 20)


def array(*shape, dtype=jnp.bfloat16):
    return jax.ShapeDtypeStruct(shape, dtype)


def position():
    return lax.axis_index("frame") // (lax.axis_size("frame") // 4)


def odd_row():
    return lax.axis_index("row") % 2


def lead(frames):
    def body(src, two, held, wide, sems):
        copies = []
        for k in range(PIECES):
            some = pl.ds(k * CH // PIECES, CH // PIECES)
            copies.append(pltpu.make_async_copy(src.at[position() ^ 2, some], held.at[some], sems.at[k]))
            copies[k].start()
        for copy in copies:
            copy.wait()
        rows_first(held[...], wide, two)

    return pl.pallas_call(
        body,
        out_shape=array(ROWS, CH, LANES),
        in_specs=[pl.BlockSpec(memory_space=pl.ANY)],
        out_specs=VMEM,
        scratch_shapes=[
            pltpu.VMEM((CH, ROWS, LANES), jnp.bfloat16),
            pltpu.VMEM((CH * ROWS, LANES), jnp.float32),
            pltpu.SemaphoreType.DMA((PIECES,)),
        ],
        compiler_params=pltpu.CompilerParams(vmem_limit_bytes=FRONT << 10),
        name="lead",
    )(frames)


def rows_first(frame, wide, out):
    wide[...] = frame.astype(jnp.float32).reshape(CH * ROWS, LANES)
    turn = 7 - 7 * odd_row()
    sign = 2 * odd_row() - 1
    for row in range(ROWS):
        out[turn + sign * row] = wide[pl.ds(row, CH, stride=ROWS), :].astype(jnp.bfloat16)


def spread(frames):
    def body(src, own, one, three, wide):
        at = position()
        for k, out in ((1, one), (3, three), (0, own)):
            rows_first(src[at ^ k], wide.at[k], out)

    return pl.pallas_call(
        body,
        out_shape=(array(ROWS, CH, LANES),) * 3,
        in_specs=[VMEM],
        out_specs=(VMEM,) * 3,
        scratch_shapes=[pltpu.VMEM((4, CH * ROWS, LANES), jnp.float32)],
        compiler_params=SMALL,
        name="spread",
    )(frames)


def weights(w_pair, w_mixed):
    def body(wp, wm, pair, mixed):
        top = 2 - 2 * odd_row()
        taps = (top, 1, 2 - top)
        for ky in range(3):
            at = ky * 2 * CH
            tap = wp[taps[ky]]
            pair[0, :, at : at + 2 * CH] = tap
            pair[1, :, at : at + 2 * CH] = jnp.concatenate([tap[:, CH:], tap[:, :CH]], axis=1)
        mixed[...] = jnp.concatenate([wm[taps[0]], wm[1], wm[taps[2]]], axis=1)

    return pl.pallas_call(
        body,
        out_shape=(array(2, 3 * CH, 6 * CH), array(3 * CH, 3 * CH)),
        in_specs=[VMEM] * 2,
        out_specs=(VMEM,) * 2,
        compiler_params=SMALL,
        name="weights",
    )(w_pair.reshape(3, 3 * CH, 2 * CH), w_mixed.reshape(3, 3 * CH, CH))


def edges(*frames):
    def body(*refs):
        near_side, far_side = refs[-2:]
        for k, frame in enumerate(refs[:-2]):
            for row in range(HALO):
                near_side[row, k * CH : (k + 1) * CH, :] = frame[HALO - 1 - row]
                far_side[row, k * CH : (k + 1) * CH, :] = frame[ROWS - 1 - row]

    half = array(HALO, len(frames) * CH, LANES)
    return pl.pallas_call(
        body,
        out_shape=(half, half),
        in_specs=[VMEM] * len(frames),
        out_specs=(VMEM,) * 2,
        compiler_params=SMALL,
        name="edges",
    )(*frames)


def fill(stack, slot, source, at, part=0):
    to = slice(slot * CH, (slot + 1) * CH)
    stack[at : at + source.shape[0], to, :] = source[:, part * CH : (part + 1) * CH, :]


def at_seam():
    row = lax.axis_index("row")
    half = lax.axis_size("row") // 2
    return (row == half) | (row == half - 1)


class Level:
    def __init__(self, pair, mixed, sp, sm, swap, hid):
        lane = lax.broadcasted_iota(jnp.int32, (CH, LANES), 1)
        self.not_first = lane > 0
        self.not_last = lane < LANES - 1
        self.pair = pair[swap]
        self.mixed = mixed[...]
        square = lax.broadcasted_iota(jnp.int32, (CH, CH), 0) == lax.broadcasted_iota(jnp.int32, (CH, CH), 1)
        self.cols = [
            jnp.broadcast_to(jnp.sum(jnp.where(square, slope[...], 0.0), axis=1, keepdims=True), (CH, LANES))
            for slope in (sp, sm)
        ]
        self.swap = swap
        self.hid = hid
        place = lax.axis_index("row")
        self.edge = (place == 0) | (place == lax.axis_size("row") - 1)

    def inside(self, row, value):
        return jnp.where(self.edge, 0.0, value) if row >= HALO + ROWS else value

    def fold(self, part, which):
        left = jnp.where(self.not_first, pltpu.roll(part[:CH], 1, 1), 0.0)
        right = jnp.where(self.not_last, pltpu.roll(part[2 * CH :], LANES - 1, 1), 0.0)
        total = part[CH : 2 * CH] + left + right
        return jnp.maximum(total, self.cols[which] * total)

    def product(self, lhs, stack, row, depth):
        rhs = jnp.concatenate([stack[r - 1 : r + 2].reshape(3 * depth, LANES) for r in (row, row + 1)], axis=1)
        return jnp.dot(lhs, rhs, preferred_element_type=jnp.float32)

    def first(self, stack, shift, low, high):
        for row in range(low, high, 2):
            both = self.product(self.pair, stack, row - shift, 2 * CH)
            for k in range(2):
                value = self.fold(both[:, k * LANES : (k + 1) * LANES], 0)
                self.hid[row + k] = self.inside(row + k, value).astype(jnp.bfloat16)

    def second(self, stack, shift, low, high, emit):
        for row in range(low, high, 2):
            both = self.product(self.mixed, self.hid, row, CH)
            for k in range(2):
                start = stack[row + k - shift, pl.ds(self.swap * CH, CH), :].astype(jnp.float32)
                branch = self.fold(both[:, k * LANES : (k + 1) * LANES], 1)
                emit(row + k, self.inside(row + k, start + branch))


def into(target, shift, to):
    def emit(row, value):
        target[row - shift, to, :] = value.astype(target.dtype)

    return emit


OTHER = slice(CH, 2 * CH)
HIDDEN = pltpu.VMEM((16, CH, LANES), jnp.bfloat16)
STACK = pltpu.VMEM((16, 2 * CH, LANES), jnp.bfloat16)


def merge_own(near_side, far_side, own, two, tables):
    def body(near_r, far_r, own_r, two_r, pair, mixed, sp, sm, out, stack, hid):
        for slot, frame in enumerate((own_r, two_r)):
            fill(stack, slot, near_r, 0, slot)
            fill(stack, slot, frame, HALO)
            fill(stack, slot, far_r, HALO + ROWS, slot)
        level = Level(pair, mixed, sp, sm, position() // 2, hid)
        level.first(stack, 0, 1, 15)
        level.second(stack, 0, 2, 14, into(out, 2, slice(None)))

    return pl.pallas_call(
        body,
        out_shape=array(12, CH, LANES),
        in_specs=[VMEM] * 8,
        out_specs=VMEM,
        scratch_shapes=[STACK, HIDDEN],
        compiler_params=SMALL,
        name="merge_own",
    )(near_side, far_side, own, two, *tables)


def merge_inner(near_side, one, three, mine, tables):
    def body(*refs):
        pl.when(at_seam())(partial(inner, *refs))

    def inner(near_r, one_r, three_r, mine_r, pair, mixed, sp, sm, hid_end, ones_end, top_end, done, stack, ones, hid, top_hid):
        for slot, frame in enumerate((one_r, three_r)):
            fill(stack, slot, near_r, 0, slot)
            fill(stack, slot, frame, HALO)
        fill(ones, 0, mine_r.at[0:8], 2)
        at = position()
        level = Level(pair, mixed, sp, sm, at // 2, hid)
        level.first(stack, 0, 1, 11)
        level.second(stack, 0, 2, 10, into(ones, 0, OTHER))
        top = Level(pair, mixed, sp, sm, at % 2, top_hid)
        top.first(ones, 0, 3, 9)
        top.second(ones, 0, 4, 8, into(done, 4, slice(None)))
        hid_end[...] = hid[9:11]
        ones_end[...] = ones[8:10]
        top_end[...] = top_hid[7:9]

    return pl.pallas_call(
        body,
        out_shape=(array(2, CH, LANES), array(2, 2 * CH, LANES), array(2, CH, LANES), array(4, CH, LANES, dtype=jnp.float32)),
        in_specs=[VMEM] * 8,
        out_specs=(VMEM,) * 4,
        scratch_shapes=[STACK, STACK, HIDDEN, HIDDEN],
        compiler_params=SMALL,
        name="merge_inner",
    )(near_side, one, three, mine, *tables)


def merge_outer(near_side, far_side, one, three, mine, inner, tables):
    def body(near_r, far_r, one_r, three_r, mine_r, hid_end, ones_end, top_end, done, pair, mixed, sp, sm, out, stack, ones, hid, top_hid, rows, wide):
        at = position()

        @pl.when(at_seam())
        def _():
            for slot, frame in enumerate((one_r, three_r)):
                fill(stack, slot, frame.at[6:8], 10)
                fill(stack, slot, far_r, HALO + ROWS, slot)
            hid[9:11] = hid_end[...]
            ones[8:10] = ones_end[...]
            fill(ones, 0, mine_r.at[8:12], 10)
            top_hid[7:9] = top_end[...]
            rows[0:4] = done[...]
            level = Level(pair, mixed, sp, sm, at // 2, hid)
            level.first(stack, 0, 11, 15)
            level.second(stack, 0, 10, 14, into(ones, 0, OTHER))
            top = Level(pair, mixed, sp, sm, at % 2, top_hid)
            top.first(ones, 0, 9, 13)
            top.second(ones, 0, 8, 12, into(rows, 4, slice(None)))

        @pl.when(jnp.logical_not(at_seam()))
        def _():
            for slot, frame in enumerate((one_r, three_r)):
                fill(stack, slot, near_r, 0, slot)
                fill(stack, slot, frame, HALO)
                fill(stack, slot, far_r, HALO + ROWS, slot)
            fill(ones, 0, mine_r, 2)
            level = Level(pair, mixed, sp, sm, at // 2, hid)
            level.first(stack, 0, 1, 15)
            level.second(stack, 0, 2, 14, into(ones, 0, OTHER))
            top = Level(pair, mixed, sp, sm, at % 2, top_hid)
            top.first(ones, 0, 3, 13)
            top.second(ones, 0, 4, 12, into(rows, 4, slice(None)))

        turn = 7 - 7 * odd_row()
        sign = 2 * odd_row() - 1
        for row in range(ROWS):
            wide[pl.ds(row, CH, stride=ROWS), :] = rows[turn + sign * row]
        out[...] = wide[...].reshape(CH, ROWS, LANES).astype(jnp.bfloat16)

    return pl.pallas_call(
        body,
        out_shape=array(CH, ROWS, LANES),
        in_specs=[VMEM] * 13,
        scratch_shapes=[
            STACK,
            STACK,
            HIDDEN,
            HIDDEN,
            pltpu.VMEM((ROWS, CH, LANES), jnp.float32),
            pltpu.VMEM((CH * ROWS, LANES), jnp.float32),
        ],
        compiler_params=SMALL,
        name="merge_outer",
    )(near_side, far_side, one, three, mine, *inner, *tables)


def on_device(frames, w_pair, w_mixed, slope_pair, slope_mixed):
    count = lax.axis_size("frame")
    quarter = count // 4
    rows = lax.axis_size("row")

    def swapped(block, mask):
        return lax.ppermute(block, "frame", [(i, i ^ (mask * quarter)) for i in range(count)])

    def on_chip(block):
        return lax.ppermute(block, "row", [(i, i ^ 1) for i in range(rows)])

    def off_chip(block):
        return lax.ppermute(block, "row", [(i, ((i + 1) ^ 1) - 1) for i in range(1, rows - 1)])

    two = lead(frames)
    own, one, three = spread(frames)
    one = swapped(one, 1)
    three = swapped(three, 3)
    two = swapped(two, 2)
    tables = (*weights(w_pair, w_mixed), slope_pair.reshape(1, CH), slope_mixed.reshape(1, CH))
    near_early, far_early = edges(own, two)
    far_early = off_chip(far_early)
    near_early = on_chip(near_early)
    near_late, far_late = edges(one, three)
    far_late = off_chip(far_late)
    near_late = on_chip(near_late)
    mine = merge_own(near_early, far_early, own, two, tables)
    inner = merge_inner(near_late, one, three, mine, tables)
    merged = merge_outer(near_late, far_late, one, three, mine, inner, tables)
    return merged[None]


def solution(mesh):
    placed = (P("frame", None, "row", None), P(), P(), P(), P())
    return jax.shard_map(
        on_device,
        mesh=mesh,
        in_specs=placed,
        out_specs=P("frame", None, "row", None),
        check_vma=False,
    )
```

```python
from functools import partial

import jax
import jax.numpy as jnp
from jax import lax
from jax.experimental import pallas as pl
from jax.experimental.pallas import tpu as pltpu
from jax.sharding import PartitionSpec as P


ROWS = 8
HALO = 4
CH = 64
LANES = 128
PIECES = 8
FRONT = 54800
VMEM = pl.BlockSpec(memory_space=pltpu.VMEM)
SMALL = pltpu.CompilerParams(vmem_limit_bytes=8 << 20)


def array(*shape, dtype=jnp.bfloat16):
    return jax.ShapeDtypeStruct(shape, dtype)


def position():
    return lax.axis_index("frame") // (lax.axis_size("frame") // 4)


def odd_row():
    return lax.axis_index("row") % 2


def lead(frames):
    def body(src, two, held, wide, sems):
        copies = []
        for k in range(PIECES):
            some = pl.ds(k * CH // PIECES, CH // PIECES)
            copies.append(pltpu.make_async_copy(src.at[position() ^ 2, some], held.at[some], sems.at[k]))
            copies[k].start()
        for copy in copies:
            copy.wait()
        rows_first(held[...], wide, two)

    return pl.pallas_call(
        body,
        out_shape=array(ROWS, CH, LANES),
        in_specs=[pl.BlockSpec(memory_space=pl.ANY)],
        out_specs=VMEM,
        scratch_shapes=[
            pltpu.VMEM((CH, ROWS, LANES), jnp.bfloat16),
            pltpu.VMEM((CH * ROWS, LANES), jnp.float32),
            pltpu.SemaphoreType.DMA((PIECES,)),
        ],
        compiler_params=pltpu.CompilerParams(vmem_limit_bytes=FRONT << 10),
        name="lead",
    )(frames)


def rows_first(frame, wide, out):
    wide[...] = frame.astype(jnp.float32).reshape(CH * ROWS, LANES)
    turn = 7 - 7 * odd_row()
    sign = 2 * odd_row() - 1
    for row in range(ROWS):
        out[turn + sign * row] = wide[pl.ds(row, CH, stride=ROWS), :].astype(jnp.bfloat16)


def spread(frames):
    def body(src, own, one, three, wide):
        at = position()
        for k, out in ((1, one), (3, three), (0, own)):
            rows_first(src[at ^ k], wide.at[k], out)

    return pl.pallas_call(
        body,
        out_shape=(array(ROWS, CH, LANES),) * 3,
        in_specs=[VMEM],
        out_specs=(VMEM,) * 3,
        scratch_shapes=[pltpu.VMEM((4, CH * ROWS, LANES), jnp.float32)],
        compiler_params=SMALL,
        name="spread",
    )(frames)


def weights(w_pair, w_mixed):
    def body(wp, wm, pair, mixed):
        top = 2 - 2 * odd_row()
        taps = (top, 1, 2 - top)
        for ky in range(3):
            at = ky * 2 * CH
            tap = wp[taps[ky]]
            pair[0, :, at : at + 2 * CH] = tap
            pair[1, :, at : at + 2 * CH] = jnp.concatenate([tap[:, CH:], tap[:, :CH]], axis=1)
        mixed[...] = jnp.concatenate([wm[taps[0]], wm[1], wm[taps[2]]], axis=1)

    return pl.pallas_call(
        body,
        out_shape=(array(2, 3 * CH, 6 * CH), array(3 * CH, 3 * CH)),
        in_specs=[VMEM] * 2,
        out_specs=(VMEM,) * 2,
        compiler_params=SMALL,
        name="weights",
    )(w_pair.reshape(3, 3 * CH, 2 * CH), w_mixed.reshape(3, 3 * CH, CH))


def edges(*frames):
    def body(*refs):
        near_side, far_side = refs[-2:]
        for k, frame in enumerate(refs[:-2]):
            for row in range(HALO):
                near_side[row, k * CH : (k + 1) * CH, :] = frame[HALO - 1 - row]
                far_side[row, k * CH : (k + 1) * CH, :] = frame[ROWS - 1 - row]

    half = array(HALO, len(frames) * CH, LANES)
    return pl.pallas_call(
        body,
        out_shape=(half, half),
        in_specs=[VMEM] * len(frames),
        out_specs=(VMEM,) * 2,
        compiler_params=SMALL,
        name="edges",
    )(*frames)


def fill(stack, slot, source, at, part=0):
    to = slice(slot * CH, (slot + 1) * CH)
    stack[at : at + source.shape[0], to, :] = source[:, part * CH : (part + 1) * CH, :]


def at_seam():
    row = lax.axis_index("row")
    half = lax.axis_size("row") // 2
    return (row == half) | (row == half - 1)


def columns(*slopes):
    square = lax.broadcasted_iota(jnp.int32, (CH, CH), 0) == lax.broadcasted_iota(jnp.int32, (CH, CH), 1)
    return [
        jnp.broadcast_to(jnp.sum(jnp.where(square, slope[...], 0.0), axis=1, keepdims=True), (CH, LANES))
        for slope in slopes
    ]


class Level:
    def __init__(self, pair, mixed, cols, swap, hid):
        lane = lax.broadcasted_iota(jnp.int32, (CH, LANES), 1)
        self.not_first = lane > 0
        self.not_last = lane < LANES - 1
        self.pair = pair[swap]
        self.mixed = mixed[...]
        self.cols = cols
        self.swap = swap
        self.hid = hid
        place = lax.axis_index("row")
        self.edge = (place == 0) | (place == lax.axis_size("row") - 1)

    def inside(self, row, value):
        return jnp.where(self.edge, 0.0, value) if row >= HALO + ROWS else value

    def fold(self, part, which):
        left = jnp.where(self.not_first, pltpu.roll(part[:CH], 1, 1), 0.0)
        right = jnp.where(self.not_last, pltpu.roll(part[2 * CH :], LANES - 1, 1), 0.0)
        total = part[CH : 2 * CH] + left + right
        return jnp.maximum(total, self.cols[which] * total)

    def product(self, lhs, stack, row, depth):
        rhs = jnp.concatenate([stack[r - 1 : r + 2].reshape(3 * depth, LANES) for r in (row, row + 1)], axis=1)
        return jnp.dot(lhs, rhs, preferred_element_type=jnp.float32)

    def first(self, stack, shift, low, high):
        for row in range(low, high, 2):
            both = self.product(self.pair, stack, row - shift, 2 * CH)
            for k in range(2):
                value = self.fold(both[:, k * LANES : (k + 1) * LANES], 0)
                self.hid[row + k] = self.inside(row + k, value).astype(jnp.bfloat16)

    def second(self, stack, shift, low, high, emit):
        for row in range(low, high, 2):
            both = self.product(self.mixed, self.hid, row, CH)
            for k in range(2):
                start = stack[row + k - shift, pl.ds(self.swap * CH, CH), :].astype(jnp.float32)
                branch = self.fold(both[:, k * LANES : (k + 1) * LANES], 1)
                emit(row + k, self.inside(row + k, start + branch))


def into(target, shift, to):
    def emit(row, value):
        target[row - shift, to, :] = value.astype(target.dtype)

    return emit


OTHER = slice(CH, 2 * CH)
HIDDEN = pltpu.VMEM((16, CH, LANES), jnp.bfloat16)
STACK = pltpu.VMEM((16, 2 * CH, LANES), jnp.bfloat16)


def merge_own(near_side, far_side, own, two, tables):
    def body(near_r, far_r, own_r, two_r, pair, mixed, sp, sm, out, stack, hid):
        for slot, frame in enumerate((own_r, two_r)):
            fill(stack, slot, near_r, 0, slot)
            fill(stack, slot, frame, HALO)
            fill(stack, slot, far_r, HALO + ROWS, slot)
        cols = columns(sp, sm)
        level = Level(pair, mixed, cols, position() // 2, hid)
        level.first(stack, 0, 1, 15)
        level.second(stack, 0, 2, 14, into(out, 2, slice(None)))

    return pl.pallas_call(
        body,
        out_shape=array(12, CH, LANES),
        in_specs=[VMEM] * 8,
        out_specs=VMEM,
        scratch_shapes=[STACK, HIDDEN],
        compiler_params=SMALL,
        name="merge_own",
    )(near_side, far_side, own, two, *tables)


def merge_inner(near_side, one, three, mine, tables):
    def body(*refs):
        pl.when(at_seam())(partial(inner, *refs))

    def inner(near_r, one_r, three_r, mine_r, pair, mixed, sp, sm, hid_end, ones_end, top_end, done, stack, ones, hid, top_hid):
        for slot, frame in enumerate((one_r, three_r)):
            fill(stack, slot, near_r, 0, slot)
            fill(stack, slot, frame, HALO)
        fill(ones, 0, mine_r.at[0:8], 2)
        at = position()
        cols = columns(sp, sm)
        level = Level(pair, mixed, cols, at // 2, hid)
        level.first(stack, 0, 1, 11)
        level.second(stack, 0, 2, 10, into(ones, 0, OTHER))
        top = Level(pair, mixed, cols, at % 2, top_hid)
        top.first(ones, 0, 3, 9)
        top.second(ones, 0, 4, 8, into(done, 4, slice(None)))
        hid_end[...] = hid[9:11]
        ones_end[...] = ones[8:10]
        top_end[...] = top_hid[7:9]

    return pl.pallas_call(
        body,
        out_shape=(array(2, CH, LANES), array(2, 2 * CH, LANES), array(2, CH, LANES), array(4, CH, LANES, dtype=jnp.float32)),
        in_specs=[VMEM] * 8,
        out_specs=(VMEM,) * 4,
        scratch_shapes=[STACK, STACK, HIDDEN, HIDDEN],
        compiler_params=SMALL,
        name="merge_inner",
    )(near_side, one, three, mine, *tables)


def merge_outer(near_side, far_side, one, three, mine, inner, tables):
    def body(near_r, far_r, one_r, three_r, mine_r, hid_end, ones_end, top_end, done, pair, mixed, sp, sm, out, stack, ones, hid, top_hid, rows, wide):
        at = position()

        @pl.when(at_seam())
        def _():
            for slot, frame in enumerate((one_r, three_r)):
                fill(stack, slot, frame.at[6:8], 10)
                fill(stack, slot, far_r, HALO + ROWS, slot)
            hid[9:11] = hid_end[...]
            ones[8:10] = ones_end[...]
            fill(ones, 0, mine_r.at[8:12], 10)
            top_hid[7:9] = top_end[...]
            rows[0:4] = done[...]
            cols = columns(sp, sm)
            level = Level(pair, mixed, cols, at // 2, hid)
            level.first(stack, 0, 11, 15)
            level.second(stack, 0, 10, 14, into(ones, 0, OTHER))
            top = Level(pair, mixed, cols, at % 2, top_hid)
            top.first(ones, 0, 9, 13)
            top.second(ones, 0, 8, 12, into(rows, 4, slice(None)))

        @pl.when(jnp.logical_not(at_seam()))
        def _():
            for slot, frame in enumerate((one_r, three_r)):
                fill(stack, slot, near_r, 0, slot)
                fill(stack, slot, frame, HALO)
                fill(stack, slot, far_r, HALO + ROWS, slot)
            fill(ones, 0, mine_r, 2)
            cols = columns(sp, sm)
            level = Level(pair, mixed, cols, at // 2, hid)
            level.first(stack, 0, 1, 15)
            level.second(stack, 0, 2, 14, into(ones, 0, OTHER))
            top = Level(pair, mixed, cols, at % 2, top_hid)
            top.first(ones, 0, 3, 13)
            top.second(ones, 0, 4, 12, into(rows, 4, slice(None)))

        turn = 7 - 7 * odd_row()
        sign = 2 * odd_row() - 1
        for row in range(ROWS):
            wide[pl.ds(row, CH, stride=ROWS), :] = rows[turn + sign * row]
        out[...] = wide[...].reshape(CH, ROWS, LANES).astype(jnp.bfloat16)

    return pl.pallas_call(
        body,
        out_shape=array(CH, ROWS, LANES),
        in_specs=[VMEM] * 13,
        scratch_shapes=[
            STACK,
            STACK,
            HIDDEN,
            HIDDEN,
            pltpu.VMEM((ROWS, CH, LANES), jnp.float32),
            pltpu.VMEM((CH * ROWS, LANES), jnp.float32),
        ],
        compiler_params=SMALL,
        name="merge_outer",
    )(near_side, far_side, one, three, mine, *inner, *tables)


def on_device(frames, w_pair, w_mixed, slope_pair, slope_mixed):
    count = lax.axis_size("frame")
    quarter = count // 4
    rows = lax.axis_size("row")

    def swapped(block, mask):
        return lax.ppermute(block, "frame", [(i, i ^ (mask * quarter)) for i in range(count)])

    def on_chip(block):
        return lax.ppermute(block, "row", [(i, i ^ 1) for i in range(rows)])

    def off_chip(block):
        return lax.ppermute(block, "row", [(i, ((i + 1) ^ 1) - 1) for i in range(1, rows - 1)])

    two = lead(frames)
    own, one, three = spread(frames)
    one = swapped(one, 1)
    three = swapped(three, 3)
    two = swapped(two, 2)
    tables = (*weights(w_pair, w_mixed), slope_pair.reshape(1, CH), slope_mixed.reshape(1, CH))
    near_early, far_early = edges(own, two)
    far_early = off_chip(far_early)
    near_early = on_chip(near_early)
    near_late, far_late = edges(one, three)
    far_late = off_chip(far_late)
    near_late = on_chip(near_late)
    mine = merge_own(near_early, far_early, own, two, tables)
    inner = merge_inner(near_late, one, three, mine, tables)
    merged = merge_outer(near_late, far_late, one, three, mine, inner, tables)
    return merged[None]


def solution(mesh):
    placed = (P("frame", None, "row", None), P(), P(), P(), P())
    return jax.shard_map(
        on_device,
        mesh=mesh,
        in_specs=placed,
        out_specs=P("frame", None, "row", None),
        check_vma=False,
    )
```
